128 devices in a mesh: sec: 16 (over x, y), strip: 8 (over z, core).
Axes of the slice: x: 4, y: 4, z: 4, core: 2. Of those that a mesh axis runs over, the one named last changes fastest.
Arguments:
- start_offsets: float32 [2, 16, 768, 2048], P(None, 'sec', 'strip'), may hold values from -0.4 to 0.4
- section_flow: float32 [2, 16, 768, 2048], P(None, 'sec', 'strip'), may hold values from -1.5 to 1.5, as said below
- fixed_nodes: int32 [16, 768, 2048], P('sec', 'strip'), may hold values 0 or 1
- links_across: int32 [16, 768, 2048], P('sec', 'strip'), may hold values 0 or 1
- links_down: int32 [16, 768, 2048], P('sec', 'strip'), may hold values 0 or 1
Outputs:
- final_offsets: float32 [2, 16, 768, 2048], P(None, 'sec', 'strip')
- final_speeds: float32 [2, 16, 768, 2048], P(None, 'sec', 'strip')
The draws below stay inside these ranges and needn't reach their ends.
Inputs may be any that keep to these rules, and one draw needn't show every extreme that they name: `section_flow`: entries of section 0 take part in no spring.
All inputs are finite; a program needn't handle non-finite values. No bound on the sum of `fixed_nodes` or of `links_across` or of `links_down` on one device may be relied on, other than what follows from the above.
Results may differ from the reference program's by a relative error of at most 0.00017.
Values sent between devices are 32-bit elements; how exact they have to be, the bound alone decides.
A program may use at most 64 MiB of HBM per device.

```python
import jax
import jax.numpy as jnp
from jax import lax

COLS = 2048
SWEEPS = 2
ROUNDS = 2
SUBSTEPS = 4
SECTIONS = 16
ROWS = 768


def draw_section_flow(key, part):
    subkeys = jax.random.split(key, 1)
    section_index = jnp.arange(SECTIONS).astype(jnp.float32)
    section_ramp = 0.12 * (0.5 + section_index / max(SECTIONS - 1, 1))
    normal_part = jax.random.truncated_normal(subkeys[0], -4.0, 4.0, (2, SECTIONS, ROWS, COLS), jnp.float32)
    sample = normal_part * section_ramp[None, :, None, None]
    return sample.astype(jnp.float32)


def place_ends(result, rng, low, high):
    extent = result.shape
    place = [jax.random.randint(jax.random.fold_in(rng, axis), (), 0, extent[axis]) for axis in range(len(extent))]
    result = result.at[tuple(place)].set(low)
    longest = extent.index(max(extent))
    place[longest] = (place[longest] + 1) % extent[longest]
    return result.at[tuple(place)].set(high)


def shard_levels(stream_key, shape, cuts, least, high):
    def one(axis_at, shards_of):
        steps = jax.random.uniform(jax.random.fold_in(jax.random.fold_in(stream_key, 6), axis_at), (shards_of,), jnp.float32, least / len(cuts), high / len(cuts))
        return jnp.repeat(jnp.exp(steps), shape[axis_at] // shards_of).reshape((-1,) + (1,) * (len(shape) - axis_at - 1))

    loudness = one(*cuts[0])
    for cut in cuts[1:]:
        loudness = loudness * one(*cut)
    return loudness


def centred(stream_key, dims, width, bound, cuts=(), kind=jnp.bfloat16):
    gain = shard_levels(stream_key, dims, cuts, -0.22, 0.18) if cuts else 1.0
    result = jax.random.normal(stream_key, dims, jnp.float32) * width * gain
    return jnp.minimum(jnp.maximum(result, -bound), bound).astype(kind)


def setup_inputs(seed: int = 0) -> dict:
    splits = jax.random.split(jax.random.key(seed), 6)
    return {
        "start_offsets": centred(splits[0], (2, SECTIONS, ROWS, COLS), 0.08, 0.4, ((1, 16), (2, 8)), jnp.float32),
        "section_flow": draw_section_flow(jax.random.fold_in(splits[5], 71), 0),
        "fixed_nodes": place_ends((jax.random.randint(splits[2], (SECTIONS, ROWS, COLS), 0, 16) < 1).astype(jnp.int32), jax.random.fold_in(splits[2], 1), 0, 1),
        "links_across": place_ends((jax.random.randint(splits[3], (SECTIONS, ROWS, COLS), 0, 16) < 15).astype(jnp.int32), jax.random.fold_in(splits[3], 1), 0, 1),
        "links_down": place_ends((jax.random.randint(splits[4], (SECTIONS, ROWS, COLS), 0, 16) < 15).astype(jnp.int32), jax.random.fold_in(splits[4], 1), 0, 1),
    }


SPRING = 1.0
COUPLING = 0.5
STEP_SIZE = 0.4
DAMPING = 0.9
SPEED_CAP = 0.05
EPSILON = 1e-06

def along_cols(values, lower, upper):
    widths = [(0, 0)] * (values.ndim - 1) + [(lower, upper)]
    return jnp.pad(values, widths)

def along_rows(values, lower, upper):
    widths = [(0, 0)] * (values.ndim - 2) + [(lower, upper), (0, 0)]
    return jnp.pad(values, widths)

def spring_forces(offsets, across, down):
    across_x = offsets[0, ..., 1:] - offsets[0, ..., :-1] + 1.0
    across_y = offsets[1, ..., 1:] - offsets[1, ..., :-1]
    tension = 0.5 * SPRING * (across_x * across_x + across_y * across_y - 1.0) * across[..., :-1]
    force_x = along_cols(tension * across_x, 0, 1) - along_cols(tension * across_x, 1, 0)
    force_y = along_cols(tension * across_y, 0, 1) - along_cols(tension * across_y, 1, 0)
    down_x = offsets[0, ..., 1:, :] - offsets[0, ..., :-1, :]
    down_y = offsets[1, ..., 1:, :] - offsets[1, ..., :-1, :] + 1.0
    strain = 0.5 * SPRING * (down_x * down_x + down_y * down_y - 1.0) * down[..., :-1, :]
    force_x = force_x + along_rows(strain * down_x, 0, 1) - along_rows(strain * down_x, 1, 0)
    force_y = force_y + along_rows(strain * down_y, 0, 1) - along_rows(strain * down_y, 1, 0)
    return jnp.stack([force_x, force_y])

def advance(offsets, speeds, across, down, mobility, target, section_links):
    force = spring_forces(offsets, across, down) + COUPLING * (target - section_links * offsets)
    speeds = mobility * (DAMPING * speeds + STEP_SIZE * force)
    return (offsets + STEP_SIZE * speeds, speeds)

def reference(start_offsets, section_flow, fixed_nodes, links_across, links_down):
    column_index = jnp.arange(COLS)
    row_index = jnp.arange(ROWS)
    across = links_across.astype(jnp.float32) * (column_index < COLS - 1).astype(jnp.float32)
    down = links_down.astype(jnp.float32) * (row_index < ROWS - 1).astype(jnp.float32)[:, None]
    mobility = 1.0 - fixed_nodes.astype(jnp.float32)
    section_index = jnp.arange(SECTIONS)
    has_below = (section_index > 0).astype(jnp.float32)
    has_above = (section_index < SECTIONS - 1).astype(jnp.float32)
    section_links = has_below + has_above
    offsets = start_offsets
    speeds = jnp.zeros_like(start_offsets)
    empty = jnp.zeros_like(start_offsets[:, :1])

    def relax(section_item):
        here_offsets, here_speeds, here_across, here_down, here_mobility, here_target, here_links = section_item
        for substep_id in range(SUBSTEPS):
            here_offsets, here_speeds = advance(here_offsets, here_speeds, here_across, here_down, here_mobility, here_target, here_links)
        return (here_offsets, here_speeds)
    for sweep_id in range(SWEEPS):
        below = jnp.concatenate([empty, offsets[:, :-1]], axis=1) + section_flow
        above = jnp.concatenate([offsets[:, 1:] - section_flow[:, 1:], empty], axis=1)
        target = has_below[:, None, None] * below + has_above[:, None, None] * above
        for round_id in range(ROUNDS):
            power = jnp.sum(speeds * speeds)
            spread = jnp.sqrt(power / (2.0 * SECTIONS * ROWS * COLS) + EPSILON)
            speeds = speeds * jnp.minimum(1.0, SPEED_CAP / spread)
            moved = lax.map(relax, (jnp.moveaxis(offsets, 1, 0), jnp.moveaxis(speeds, 1, 0), across, down, mobility, jnp.moveaxis(target, 1, 0), section_links))
            offsets = jnp.moveaxis(moved[0], 0, 1)
            speeds = jnp.moveaxis(moved[1], 0, 1)
    return (offsets, speeds)
```

```python
import functools

import jax
import jax.numpy as jnp
from jax import lax
from jax.experimental import pallas as pl
from jax.experimental.pallas import tpu as pltpu
from jax.sharding import PartitionSpec as P

SPRING = 1.0
COUPLING = 0.5
STEP_SIZE = 0.4
DAMPING = 0.9
SPEED_CAP = 0.05
EPSILON = 1e-06
SUBSTEPS = 4

LINK = 0.5 * SPRING * STEP_SIZE * STEP_SIZE
PULL = COUPLING * STEP_SIZE * STEP_SIZE

HALO = 8
SUB = 8
LANES = 128
WIDE = 2
MESH = pl.DeviceIdType.MESH


def vreg_iota(axis):
    return lax.broadcasted_iota(jnp.int32, (SUB, LANES), axis)


def kernel(
    ns, nz, rows, tiles_c,
    u0, flow, fixed, links_a, links_d, out_u, out_v,
    sa, sb, sc, tgt, coef, raw, fl, sd, rx, carry, acc, mine, red1, red2,
    ld_u, ld_f, ld_g, e_snd, e_rcv, th_snd, th_rcv, h0_snd, h0_rcv, h1_snd, h1_rcv,
    r1_snd, r1_rcv, r2_snd, r2_rcv, out_sem,
):
    nc = tiles_c // WIDE
    nt = (rows + 2 * HALO) // SUB
    sec = lax.axis_index("sec")
    strip = lax.axis_index("strip")
    sec_up, sec_dn = lax.rem(sec + 1, ns), lax.rem(sec + ns - 1, ns)
    has_above_strip, has_below_strip = strip > 0, strip < nz - 1
    own = pl.ds(HALO, rows)

    def start_u(j, _):
        cols = pl.ds(pl.multiple_of(j * LANES, LANES), LANES)
        pltpu.make_async_copy(u0.at[:, 0, :, cols], sa.at[0:2, j, own, :], ld_u.at[j]).start()
        pltpu.make_async_copy(flow.at[:, 0, :, cols], fl.at[:, j], ld_f.at[j]).start()
        return 0

    def start_g(j, _):
        cols = pl.ds(pl.multiple_of(j * LANES, LANES), LANES)
        for n, ref in enumerate((links_a, links_d, fixed)):
            pltpu.make_async_copy(ref.at[0, :, cols], raw.at[n, j, own, :], ld_g.at[n, j]).start()
        return 0

    lax.fori_loop(0, tiles_c, start_u, 0)
    lax.fori_loop(0, tiles_c, start_g, 0)

    barrier = pltpu.get_barrier_semaphore()

    def greet_strip(d, _):
        pl.semaphore_signal(barrier, inc=1, device_id={"strip": lax.rem(strip + d, nz)}, device_id_type=MESH)
        return 0

    def greet_sec(d, _):
        pl.semaphore_signal(barrier, inc=1, device_id={"sec": lax.rem(sec + d, ns)}, device_id_type=MESH)
        return 0

    lax.fori_loop(1, nz, greet_strip, 0)
    lax.fori_loop(1, ns, greet_sec, 0)

    zero = jnp.zeros((SUB, LANES), jnp.float32)
    zero_i = jnp.zeros((SUB, LANES), jnp.int32)

    def clear(at):
        def body(j, _):
            for n in range(3):
                raw[n, j, at, :] = zero_i
            for n in range(2):
                sa[n, j, at, :] = zero
                tgt[0, n, j, at, :] = zero
                tgt[1, n, j, at, :] = zero
            for n in range(4):
                sc[n, j, at, :] = zero
            return 0

        lax.fori_loop(0, tiles_c, body, 0)

    top_halo, bottom_halo = pl.ds(0, HALO), pl.ds(HALO + rows, HALO)
    top_own, bottom_own = pl.ds(HALO, HALO), pl.ds(rows, HALO)

    @pl.when(jnp.logical_not(has_above_strip))
    def _():
        clear(top_halo)

    @pl.when(jnp.logical_not(has_below_strip))
    def _():
        clear(bottom_halo)

    pl.semaphore_wait(barrier, nz - 1 + ns - 1)

    pieces = ((0, SUB), (rows - SUB, SUB), (SUB, rows - 2 * SUB))

    def e_copy(sweep, d, c, p, state):
        first, count = pieces[p]
        chunk = pl.ds(c * WIDE, WIDE)
        if d == 0:
            src = state.at[0:2, chunk, pl.ds(HALO + first, count), :]
        else:
            src = sd.at[sweep, :, chunk, pl.ds(first, count), :]
        return pltpu.make_async_remote_copy(
            src_ref=src,
            dst_ref=rx.at[sweep, d, :, chunk, pl.ds(first, count), :],
            send_sem=e_snd.at[sweep, d, c, p],
            recv_sem=e_rcv.at[sweep, d, c, p],
            device_id={"sec": sec_up if d == 0 else sec_dn},
            device_id_type=MESH,
        )

    def strip_copy(ref_of, d, snd, rcv):
        return pltpu.make_async_remote_copy(
            src_ref=ref_of(top_own if d == 0 else bottom_own),
            dst_ref=ref_of(bottom_halo if d == 0 else top_halo),
            send_sem=snd,
            recv_sem=rcv,
            device_id={"strip": strip + (-1 if d == 0 else 1)},
            device_id_type=MESH,
        )

    sends_to = (has_above_strip, has_below_strip)
    hears_from = (has_below_strip, has_above_strip)

    def strip_start(make):
        for d in range(2):
            @pl.when(sends_to[d])
            def _():
                make(d).start()

    def strip_wait_send(make):
        for d in range(2):
            @pl.when(sends_to[d])
            def _():
                make(d).wait_send()

    def strip_wait_recv(make):
        for d in range(2):
            @pl.when(hears_from[d])
            def _():
                make(d).wait_recv()

    def t_halo(sweep, c):
        chunk = pl.ds(c * WIDE, WIDE)
        return lambda d: strip_copy(
            lambda at: tgt.at[sweep, :, chunk, at, :], d, th_snd.at[sweep, d, c], th_rcv.at[sweep, d, c]
        )

    def u_halo(d):
        return strip_copy(lambda at: sa.at[0:2, :, at, :], d, h0_snd.at[0, d], h0_rcv.at[0, d])

    def raw_halo(d):
        return strip_copy(lambda at: raw.at[:, :, at, :], d, h0_snd.at[1, d], h0_rcv.at[1, d])

    def s_halo(c):
        chunk = pl.ds(c * WIDE, WIDE)
        return lambda d: strip_copy(
            lambda at: sc.at[:, chunk, at, :], d, h1_snd.at[d, c], h1_rcv.at[d, c]
        )

    def make_down(sweep, c, state):
        for jj in range(WIDE):
            j = c * WIDE + jj
            for n in range(2):
                sd[sweep, n, j] = state[n, j, own, :] - fl[n, j]

    def e_send(sweep, c, state):
        for d in range(2):
            for p in range(3):
                e_copy(sweep, d, c, p, state).start()

    def first_sends(c, _):
        for jj in range(WIDE):
            j = c * WIDE + jj
            cols = pl.ds(pl.multiple_of(j * LANES, LANES), LANES)
            pltpu.make_async_copy(u0.at[:, 0, :, cols], sa.at[0:2, j, own, :], ld_u.at[j]).wait()
            pltpu.make_async_copy(flow.at[:, 0, :, cols], fl.at[:, j], ld_f.at[j]).wait()
        make_down(0, c, sa)
        e_send(0, c, sa)
        return 0

    lax.fori_loop(0, nc, first_sends, 0)
    strip_start(u_halo)

    def wait_g(j, _):
        cols = pl.ds(pl.multiple_of(j * LANES, LANES), LANES)
        for n, ref in enumerate((links_a, links_d, fixed)):
            pltpu.make_async_copy(ref.at[0, :, cols], raw.at[n, j, own, :], ld_g.at[n, j]).wait()
        return 0

    lax.fori_loop(0, tiles_c, wait_g, 0)
    strip_start(raw_halo)
    strip_wait_recv(u_halo)
    strip_wait_recv(raw_halo)

    lane, sublane = vreg_iota(1), vreg_iota(0)
    first_lane, last_lane = lane == 0, lane == LANES - 1
    first_sub = sublane == 0

    def convert(j, _):
        edge = jnp.logical_and(last_lane, j == tiles_c - 1)
        for i in range(nt):
            at = pl.ds(SUB * i, SUB)
            a = raw[0, j, at, :].astype(jnp.float32) * LINK
            coef[0, j, at, :] = jnp.where(edge, 0.0, a)
            dn = raw[1, j, at, :].astype(jnp.float32) * LINK
            if SUB * i == rows:
                bottom = jnp.logical_and(sublane == SUB - 1, strip == nz - 1)
                dn = jnp.where(bottom, 0.0, dn)
            coef[1, j, at, :] = dn
            coef[2, j, at, :] = 1.0 - raw[2, j, at, :].astype(jnp.float32)
        return 0

    lax.fori_loop(0, tiles_c, convert, 0)

    has_below, has_above = sec > 0, sec < ns - 1
    links = has_below.astype(jnp.float32) + has_above.astype(jnp.float32)
    hold = jnp.full((SUB, LANES), PULL, jnp.float32) * links
    below_on = jnp.broadcast_to(has_below, (SUB, LANES))
    above_on = jnp.broadcast_to(has_above, (SUB, LANES))

    def make_target(sweep, c, first, count):
        for jj in range(WIDE):
            j = c * WIDE + jj
            for i in range(first // SUB, (first + count) // SUB):
                at = pl.ds(SUB * i, SUB)
                for n in range(2):
                    below = jnp.where(below_on, rx[sweep, 0, n, j, at, :] + fl[n, j, at, :], 0.0)
                    above = jnp.where(above_on, rx[sweep, 1, n, j, at, :], 0.0)
                    tgt[sweep, n, j, pl.ds(HALO + SUB * i, SUB), :] = (below + above) * PULL

    def level(k, c, src, dst, sweep, damping, own_rows, power, final):
        lo, hi = (HALO // SUB, nt - HALO // SUB) if own_rows else (0, nt)
        j0 = c * WIDE
        beyond = jnp.minimum(j0 + WIDE, tiles_c - 1)
        js = [j0 + jj for jj in range(WIDE)] + [beyond]
        up_x, up_y = [zero] * WIDE, [zero] * WIDE
        total = zero

        def down_pull(i, jj, ux, uy):
            after = pl.ds(SUB * i + 1, SUB)
            dx = src[0, js[jj], after, :] - ux
            dy = src[1, js[jj], after, :] - uy
            ey = dy + 1.0
            stretch = dx * dx + dy * (ey + 1.0)
            pull = stretch * coef[1, js[jj], pl.ds(SUB * i, SUB), :]
            return pull * dx, pull * ey

        if own_rows:
            at = pl.ds(SUB * (lo - 1), SUB)
            for jj in range(WIDE):
                hx, hy = down_pull(lo - 1, jj, src[0, js[jj], at, :], src[1, js[jj], at, :])
                up_x[jj], up_y[jj] = pltpu.roll(hx, 1, 0), pltpu.roll(hy, 1, 0)
        for i in range(lo, hi):
            at = pl.ds(SUB * i, SUB)
            ux = [src[0, j, at, :] for j in js]
            uy = [src[1, j, at, :] for j in js]
            turned_x = [pltpu.roll(u, LANES - 1, 1) for u in ux]
            turned_y = [pltpu.roll(u, LANES - 1, 1) for u in uy]
            left_x, left_y = carry[k, 0, at, :], carry[k, 1, at, :]
            for jj in range(WIDE):
                j = js[jj]
                dx = jnp.where(last_lane, turned_x[jj + 1], turned_x[jj]) - ux[jj]
                dy = jnp.where(last_lane, turned_y[jj + 1], turned_y[jj]) - uy[jj]
                ex = dx + 1.0
                pull = (dx * (ex + 1.0) + dy * dy) * coef[0, j, at, :]
                ax, ay = pull * ex, pull * dy
                gx, gy = pltpu.roll(ax, 1, 1), pltpu.roll(ay, 1, 1)
                fx = ax - jnp.where(first_lane, left_x, gx)
                fy = ay - jnp.where(first_lane, left_y, gy)
                left_x, left_y = gx, gy
                hx, hy = down_pull(i, jj, ux[jj], uy[jj])
                vx, vy = pltpu.roll(hx, 1, 0), pltpu.roll(hy, 1, 0)
                fx = fx + (hx - jnp.where(first_sub, up_x[jj], vx))
                fy = fy + (hy - jnp.where(first_sub, up_y[jj], vy))
                up_x[jj], up_y[jj] = vx, vy
                fx = fx + (tgt[sweep, 0, j, at, :] - hold * ux[jj])
                fy = fy + (tgt[sweep, 1, j, at, :] - hold * uy[jj])
                if damping is not None:
                    fx = fx + damping * src[2, j, at, :]
                    fy = fy + damping * src[3, j, at, :]
                mobility = coef[2, j, at, :]
                wx, wy = mobility * fx, mobility * fy
                dst[0, j, at, :] = ux[jj] + wx
                dst[1, j, at, :] = uy[jj] + wy
                if final:
                    dst[2, j, at, :] = wx * (1.0 / STEP_SIZE)
                    dst[3, j, at, :] = wy * (1.0 / STEP_SIZE)
                else:
                    dst[2, j, at, :] = wx
                    dst[3, j, at, :] = wy
                if power and HALO // SUB <= i < nt - HALO // SUB:
                    total = total + (wx * wx + wy * wy)
            carry[k, 0, at, :] = left_x
            carry[k, 1, at, :] = left_y
        if power:
            acc[...] += total

    def reset():
        for k in range(SUBSTEPS):
            for n in range(2):
                for i in range(nt):
                    carry[k, n, pl.ds(SUB * i, SUB), :] = zero
        acc[...] = zero

    def chunk_in(c):
        return jnp.logical_and(c >= 0, c < nc)

    entries = 2.0 * ns * nz * rows * tiles_c * LANES

    def spread_scale(n):
        mine[2 * n] = jnp.sum(acc[...], axis=0, keepdims=True)

        def to_strip(d):
            return pltpu.make_async_remote_copy(
                src_ref=mine.at[2 * n], dst_ref=red1.at[n, d - 1],
                send_sem=r1_snd.at[n, d - 1], recv_sem=r1_rcv.at[n, d - 1],
                device_id={"strip": lax.rem(strip + d, nz)}, device_id_type=MESH,
            )

        def to_sec(d):
            return pltpu.make_async_remote_copy(
                src_ref=mine.at[2 * n + 1], dst_ref=red2.at[n, d - 1],
                send_sem=r2_snd.at[n, d - 1], recv_sem=r2_rcv.at[n, d - 1],
                device_id={"sec": lax.rem(sec + d, ns)}, device_id_type=MESH,
            )

        for d in range(1, nz):
            to_strip(d).start()
        for d in range(1, nz):
            to_strip(d).wait_recv()
        mine[2 * n + 1] = mine[2 * n] + jnp.sum(red1[n], axis=0)
        for d in range(1, ns):
            to_sec(d).start()
        for d in range(1, ns):
            to_sec(d).wait_recv()
        whole = mine[2 * n + 1] + jnp.sum(red2[n], axis=0)
        for d in range(1, nz):
            to_strip(d).wait_send()
        for d in range(1, ns):
            to_sec(d).wait_send()
        power = jnp.sum(whole, axis=1, keepdims=True) * (1.0 / (STEP_SIZE * STEP_SIZE))
        spread = jnp.sqrt(power * (1.0 / entries) + EPSILON)
        scale = jnp.minimum(1.0, SPEED_CAP / spread)
        return jnp.broadcast_to(scale * DAMPING, (SUB, LANES))

    plain = DAMPING

    def wave(w, order, sweep, first_damping, own_rows, final=False, power=True, before=None):
        for k in range(SUBSTEPS):
            c = w - k
            last = k == SUBSTEPS - 1

            @pl.when(chunk_in(c))
            def _():
                if before is not None and k == 1:
                    before(c)
                level(
                    k, c, order[k], order[k + 1], sweep,
                    first_damping if k == 0 else plain,
                    own_rows and last, power and last, final and last,
                )

    def targets(w, sweep, state):
        @pl.when(w < nc)
        def _():
            for p in range(2):
                for d in range(2):
                    e_copy(sweep, d, w, p, state).wait_recv()
            for p in range(2):
                make_target(sweep, w, *pieces[p])
            strip_start(t_halo(sweep, w))

        @pl.when(chunk_in(w - 1))
        def _():
            c = w - 1
            for d in range(2):
                e_copy(sweep, d, c, 2, state).wait_recv()
            make_target(sweep, c, *pieces[2])
            strip_wait_recv(t_halo(sweep, c))

    def sent(sweep, state):
        def before(c):
            for d in range(2):
                for p in range(3):
                    e_copy(sweep, d, c, p, state).wait_send()
            if sweep == 1:
                strip_wait_send(s_halo(c))

        return before

    reset()
    strip_wait_send(u_halo)
    strip_wait_send(raw_halo)

    def round0(w, _):
        targets(w, 0, sa)
        wave(w - 1, (sa, sb, sa, sb, sa), 0, None, False, before=sent(0, sa))
        return 0

    lax.fori_loop(0, nc + SUBSTEPS, round0, 0)
    damping1 = spread_scale(0)

    reset()

    def round1(w, _):
        wave(w, (sa, sb, sa, sb, sc), 0, damping1, True)
        c = w - (SUBSTEPS - 1)

        @pl.when(chunk_in(c))
        def _():
            make_down(1, c, sc)
            strip_start(s_halo(c))
            e_send(1, c, sc)

        return 0

    lax.fori_loop(0, nc + SUBSTEPS - 1, round1, 0)
    damping2 = spread_scale(1)

    reset()

    def round2(w, _):
        @pl.when(w < nc)
        def _():
            strip_wait_recv(s_halo(w))

        targets(w, 1, sc)
        wave(w - 1, (sc, sb, sc, sb, sc), 1, damping2, False, before=sent(1, sc))
        return 0

    lax.fori_loop(0, nc + SUBSTEPS, round2, 0)
    damping3 = spread_scale(2)

    reset()

    def out_copies(j):
        cols = pl.ds(pl.multiple_of(j * LANES, LANES), LANES)
        return (
            pltpu.make_async_copy(sa.at[0:2, j, own, :], out_u.at[:, 0, :, cols], out_sem.at[0, j]),
            pltpu.make_async_copy(sa.at[2:4, j, own, :], out_v.at[:, 0, :, cols], out_sem.at[1, j]),
        )

    def round3(w, _):
        wave(w, (sc, sb, sc, sb, sa), 1, damping3, True, final=True, power=False)
        c = w - (SUBSTEPS - 1)

        @pl.when(chunk_in(c))
        def _():
            for jj in range(WIDE):
                for copy in out_copies(c * WIDE + jj):
                    copy.start()

        return 0

    lax.fori_loop(0, nc + SUBSTEPS - 1, round3, 0)

    def finish(c, _):
        strip_wait_send(t_halo(0, c))
        strip_wait_send(t_halo(1, c))
        for jj in range(WIDE):
            for copy in out_copies(c * WIDE + jj):
                copy.wait()
        return 0

    lax.fori_loop(0, nc, finish, 0)


def relax(mesh, start_offsets, section_flow, fixed_nodes, links_across, links_down):
    ns, nz = mesh.shape["sec"], mesh.shape["strip"]
    rows, columns = fixed_nodes.shape[1:]
    tiles_c = columns // LANES
    nc = tiles_c // WIDE
    padded = rows + 2 * HALO
    f32 = jnp.float32
    state = pltpu.VMEM((4, tiles_c, padded + SUB, LANES), f32)
    dma = pltpu.SemaphoreType.DMA
    out = jax.ShapeDtypeStruct(start_offsets.shape, f32)
    return pl.pallas_call(
        functools.partial(kernel, ns, nz, rows, tiles_c),
        out_shape=(out, out),
        in_specs=[pl.BlockSpec(memory_space=pl.ANY)] * 5,
        out_specs=(pl.BlockSpec(memory_space=pl.ANY), pl.BlockSpec(memory_space=pl.ANY)),
        scratch_shapes=[
            state, state, state,
            pltpu.VMEM((2, 2, tiles_c, padded, LANES), f32),
            pltpu.VMEM((3, tiles_c, padded, LANES), f32),
            pltpu.VMEM((3, tiles_c, padded, LANES), jnp.int32),
            pltpu.VMEM((2, tiles_c, rows, LANES), f32),
            pltpu.VMEM((2, 2, tiles_c, rows, LANES), f32),
            pltpu.VMEM((2, 2, 2, tiles_c, rows, LANES), f32),
            pltpu.VMEM((SUBSTEPS, 2, padded, LANES), f32),
            pltpu.VMEM((SUB, LANES), f32),
            pltpu.VMEM((6, 1, LANES), f32),
            pltpu.VMEM((3, nz - 1, 1, LANES), f32),
            pltpu.VMEM((3, ns - 1, 1, LANES), f32),
            dma((tiles_c,)), dma((tiles_c,)), dma((3, tiles_c)),
            dma((2, 2, nc, 3)), dma((2, 2, nc, 3)),
            dma((2, 2, nc)), dma((2, 2, nc)),
            dma((2, 2)), dma((2, 2)),
            dma((2, nc)), dma((2, nc)),
            dma((3, nz - 1)), dma((3, nz - 1)),
            dma((3, ns - 1)), dma((3, ns - 1)),
            dma((2, tiles_c)),
        ],
        compiler_params=pltpu.CompilerParams(
            collective_id=0, has_side_effects=True, vmem_limit_bytes=60 * 1024 * 1024
        ),
    )(start_offsets, section_flow, fixed_nodes, links_across, links_down)


def solution(mesh):
    whole = P(None, "sec", "strip", None)
    flags = P("sec", "strip", None)
    return jax.shard_map(
        functools.partial(relax, mesh),
        mesh=mesh,
        in_specs=(whole, whole, flags, flags, flags),
        out_specs=(whole, whole),
        check_vma=False,
    )
```

```python
import functools

import jax
import jax.numpy as jnp
from jax import lax
from jax.experimental import pallas as pl
from jax.experimental.pallas import tpu as pltpu
from jax.sharding import PartitionSpec as P

SPRING = 1.0
COUPLING = 0.5
STEP_SIZE = 0.4
DAMPING = 0.9
SPEED_CAP = 0.05
EPSILON = 1e-06
SUBSTEPS = 4

LINK = 0.5 * SPRING * STEP_SIZE * STEP_SIZE
PULL = COUPLING * STEP_SIZE * STEP_SIZE

HALO = 8
SUB = 8
LANES = 128
WIDE = 2
MESH = pl.DeviceIdType.MESH


def vreg_iota(axis):
    return lax.broadcasted_iota(jnp.int32, (SUB, LANES), axis)


def kernel(
    ns, nz, rows, tiles_c,
    u0, flow, fixed, links_a, links_d, out_u, out_v,
    sa, sb, sc, tgt, coef, raw, fl, sd, rx, carry, acc, mine, red1, red2,
    ld_s, ld_g, e_snd, e_rcv, th_snd, th_rcv, h0_snd, h0_rcv, h1_snd, h1_rcv,
    r1_snd, r1_rcv, r2_snd, r2_rcv, out_sem,
):
    nc = tiles_c // WIDE
    nt = (rows + 2 * HALO) // SUB
    sec = lax.axis_index("sec")
    strip = lax.axis_index("strip")
    sec_up, sec_dn = lax.rem(sec + 1, ns), lax.rem(sec + ns - 1, ns)
    has_above_strip, has_below_strip = strip > 0, strip < nz - 1
    own = pl.ds(HALO, rows)

    def wait_bytes(ref, sem):
        pltpu.make_async_copy(ref, ref, sem).wait()

    def start_u(j, _):
        cols = pl.ds(pl.multiple_of(j * LANES, LANES), LANES)
        sem = ld_s.at[j // WIDE]
        pltpu.make_async_copy(u0.at[:, 0, :, cols], sa.at[0:2, j, own, :], sem).start()
        pltpu.make_async_copy(flow.at[:, 0, :, cols], fl.at[:, j], sem).start()
        return 0

    def start_g(j, _):
        cols = pl.ds(pl.multiple_of(j * LANES, LANES), LANES)
        for n, ref in enumerate((links_a, links_d, fixed)):
            pltpu.make_async_copy(ref.at[0, :, cols], raw.at[n, j, own, :], ld_g.at[0]).start()
        return 0

    lax.fori_loop(0, tiles_c, start_u, 0)
    lax.fori_loop(0, tiles_c, start_g, 0)

    barrier = pltpu.get_barrier_semaphore()

    def greet_strip(d, _):
        pl.semaphore_signal(barrier, inc=1, device_id={"strip": lax.rem(strip + d, nz)}, device_id_type=MESH)
        return 0

    def greet_sec(d, _):
        pl.semaphore_signal(barrier, inc=1, device_id={"sec": lax.rem(sec + d, ns)}, device_id_type=MESH)
        return 0

    lax.fori_loop(1, nz, greet_strip, 0)
    lax.fori_loop(1, ns, greet_sec, 0)

    zero = jnp.zeros((SUB, LANES), jnp.float32)
    zero_i = jnp.zeros((SUB, LANES), jnp.int32)

    def clear(at):
        def body(j, _):
            for n in range(3):
                raw[n, j, at, :] = zero_i
            for n in range(2):
                sa[n, j, at, :] = zero
                tgt[0, n, j, at, :] = zero
                tgt[1, n, j, at, :] = zero
            for n in range(4):
                sc[n, j, at, :] = zero
            return 0

        lax.fori_loop(0, tiles_c, body, 0)

    top_halo, bottom_halo = pl.ds(0, HALO), pl.ds(HALO + rows, HALO)
    top_own, bottom_own = pl.ds(HALO, HALO), pl.ds(rows, HALO)

    @pl.when(jnp.logical_not(has_above_strip))
    def _():
        clear(top_halo)

    @pl.when(jnp.logical_not(has_below_strip))
    def _():
        clear(bottom_halo)

    pieces = ((0, SUB), (rows - SUB, SUB), (SUB, rows - 2 * SUB))

    def e_copy(sweep, d, c, p, state):
        first, count = pieces[p]
        chunk = pl.ds(c * WIDE, WIDE)
        if d == 0:
            src = state.at[0:2, chunk, pl.ds(HALO + first, count), :]
        else:
            src = sd.at[sweep, :, chunk, pl.ds(first, count), :]
        return pltpu.make_async_remote_copy(
            src_ref=src,
            dst_ref=rx.at[sweep, d, :, chunk, pl.ds(first, count), :],
            send_sem=e_snd.at[d, c],
            recv_sem=e_rcv.at[d, c, p // 2],
            device_id={"sec": sec_up if d == 0 else sec_dn},
            device_id_type=MESH,
        )

    def strip_copy(ref_of, d, snd, rcv):
        return pltpu.make_async_remote_copy(
            src_ref=ref_of(top_own if d == 0 else bottom_own),
            dst_ref=ref_of(bottom_halo if d == 0 else top_halo),
            send_sem=snd,
            recv_sem=rcv,
            device_id={"strip": strip + (-1 if d == 0 else 1)},
            device_id_type=MESH,
        )

    sends_to = (has_above_strip, has_below_strip)
    hears_from = (has_below_strip, has_above_strip)

    def strip_start(make):
        for d in range(2):
            @pl.when(sends_to[d])
            def _():
                make(d).start()

    def strip_wait_send(make):
        for d in range(2):
            @pl.when(sends_to[d])
            def _():
                make(d).wait_send()

    def strip_wait_recv(make):
        for d in range(2):
            @pl.when(hears_from[d])
            def _():
                make(d).wait_recv()

    def t_halo(sweep, c):
        chunk = pl.ds(c * WIDE, WIDE)
        return lambda d: strip_copy(
            lambda at: tgt.at[sweep, :, chunk, at, :], d, th_snd.at[sweep, d], th_rcv.at[d, c]
        )

    def u_halo(d):
        return strip_copy(lambda at: sa.at[0:2, :, at, :], d, h0_snd.at[0, d], h0_rcv.at[0, d])

    def raw_halo(d):
        return strip_copy(lambda at: raw.at[:, :, at, :], d, h0_snd.at[1, d], h0_rcv.at[1, d])

    def s_halo(c):
        chunk = pl.ds(c * WIDE, WIDE)
        return lambda d: strip_copy(
            lambda at: sc.at[:, chunk, at, :], d, h1_snd.at[d], h1_rcv.at[d]
        )

    def strip_wait_all(on, ref, sem):
        for d in range(2):
            @pl.when(on[d])
            def _():
                wait_bytes(ref, sem.at[d])

    def make_down(sweep, c, state):
        for jj in range(WIDE):
            j = c * WIDE + jj
            for n in range(2):
                sd[sweep, n, j] = state[n, j, own, :] - fl[n, j]

    def e_send(sweep, c, state):
        for d in range(2):
            for p in range(3):
                e_copy(sweep, d, c, p, state).start()

    def prepare(c):
        wait_bytes(rx.at[0, :, :, pl.ds(c * WIDE, WIDE)], ld_s.at[c])
        make_down(0, c, sa)

    def first_sends(c, _):
        prepare(c)
        e_send(0, c, sa)
        return 0

    prepare(0)
    pl.semaphore_wait(barrier, nz - 1 + ns - 1)
    e_send(0, 0, sa)
    lax.fori_loop(1, nc, first_sends, 0)
    strip_start(u_halo)

    wait_bytes(raw.at[:, :, own, :], ld_g.at[0])
    strip_start(raw_halo)
    strip_wait_recv(u_halo)
    strip_wait_recv(raw_halo)

    lane, sublane = vreg_iota(1), vreg_iota(0)
    first_lane, last_lane = lane == 0, lane == LANES - 1
    first_sub = sublane == 0

    def convert(j, _):
        edge = jnp.logical_and(last_lane, j == tiles_c - 1)
        for i in range(nt):
            at = pl.ds(SUB * i, SUB)
            a = raw[0, j, at, :].astype(jnp.float32) * LINK
            coef[0, j, at, :] = jnp.where(edge, 0.0, a)
            dn = raw[1, j, at, :].astype(jnp.float32) * LINK
            if SUB * i == rows:
                bottom = jnp.logical_and(sublane == SUB - 1, strip == nz - 1)
                dn = jnp.where(bottom, 0.0, dn)
            coef[1, j, at, :] = dn
            coef[2, j, at, :] = 1.0 - raw[2, j, at, :].astype(jnp.float32)
        return 0

    lax.fori_loop(0, tiles_c, convert, 0)

    has_below, has_above = sec > 0, sec < ns - 1
    links = has_below.astype(jnp.float32) + has_above.astype(jnp.float32)
    hold = jnp.full((SUB, LANES), PULL, jnp.float32) * links
    below_on = jnp.broadcast_to(has_below, (SUB, LANES))
    above_on = jnp.broadcast_to(has_above, (SUB, LANES))

    def make_target(sweep, c, first, count):
        for jj in range(WIDE):
            j = c * WIDE + jj
            for i in range(first // SUB, (first + count) // SUB):
                at = pl.ds(SUB * i, SUB)
                for n in range(2):
                    below = jnp.where(below_on, rx[sweep, 0, n, j, at, :] + fl[n, j, at, :], 0.0)
                    above = jnp.where(above_on, rx[sweep, 1, n, j, at, :], 0.0)
                    tgt[sweep, n, j, pl.ds(HALO + SUB * i, SUB), :] = (below + above) * PULL

    def level(k, c, src, dst, sweep, damping, own_rows, power, final):
        lo, hi = (HALO // SUB, nt - HALO // SUB) if own_rows else (0, nt)
        j0 = c * WIDE
        beyond = jnp.minimum(j0 + WIDE, tiles_c - 1)
        js = [j0 + jj for jj in range(WIDE)] + [beyond]
        up_x, up_y = [zero] * WIDE, [zero] * WIDE
        total = zero

        def down_pull(i, jj, ux, uy):
            after = pl.ds(SUB * i + 1, SUB)
            dx = src[0, js[jj], after, :] - ux
            dy = src[1, js[jj], after, :] - uy
            ey = dy + 1.0
            stretch = dx * dx + dy * (ey + 1.0)
            pull = stretch * coef[1, js[jj], pl.ds(SUB * i, SUB), :]
            return pull * dx, pull * ey

        if own_rows:
            at = pl.ds(SUB * (lo - 1), SUB)
            for jj in range(WIDE):
                hx, hy = down_pull(lo - 1, jj, src[0, js[jj], at, :], src[1, js[jj], at, :])
                up_x[jj], up_y[jj] = pltpu.roll(hx, 1, 0), pltpu.roll(hy, 1, 0)
        for i in range(lo, hi):
            at = pl.ds(SUB * i, SUB)
            ux = [src[0, j, at, :] for j in js]
            uy = [src[1, j, at, :] for j in js]
            turned_x = [pltpu.roll(u, LANES - 1, 1) for u in ux]
            turned_y = [pltpu.roll(u, LANES - 1, 1) for u in uy]
            left_x, left_y = carry[k, 0, at, :], carry[k, 1, at, :]
            for jj in range(WIDE):
                j = js[jj]
                dx = jnp.where(last_lane, turned_x[jj + 1], turned_x[jj]) - ux[jj]
                dy = jnp.where(last_lane, turned_y[jj + 1], turned_y[jj]) - uy[jj]
                ex = dx + 1.0
                pull = (dx * (ex + 1.0) + dy * dy) * coef[0, j, at, :]
                ax, ay = pull * ex, pull * dy
                gx, gy = pltpu.roll(ax, 1, 1), pltpu.roll(ay, 1, 1)
                fx = ax - jnp.where(first_lane, left_x, gx)
                fy = ay - jnp.where(first_lane, left_y, gy)
                left_x, left_y = gx, gy
                hx, hy = down_pull(i, jj, ux[jj], uy[jj])
                vx, vy = pltpu.roll(hx, 1, 0), pltpu.roll(hy, 1, 0)
                fx = fx + (hx - jnp.where(first_sub, up_x[jj], vx))
                fy = fy + (hy - jnp.where(first_sub, up_y[jj], vy))
                up_x[jj], up_y[jj] = vx, vy
                fx = fx + (tgt[sweep, 0, j, at, :] - hold * ux[jj])
                fy = fy + (tgt[sweep, 1, j, at, :] - hold * uy[jj])
                if damping is not None:
                    fx = fx + damping * src[2, j, at, :]
                    fy = fy + damping * src[3, j, at, :]
                mobility = coef[2, j, at, :]
                wx, wy = mobility * fx, mobility * fy
                dst[0, j, at, :] = ux[jj] + wx
                dst[1, j, at, :] = uy[jj] + wy
                if final:
                    dst[2, j, at, :] = wx * (1.0 / STEP_SIZE)
                    dst[3, j, at, :] = wy * (1.0 / STEP_SIZE)
                else:
                    dst[2, j, at, :] = wx
                    dst[3, j, at, :] = wy
                if power and HALO // SUB <= i < nt - HALO // SUB:
                    total = total + (wx * wx + wy * wy)
            carry[k, 0, at, :] = left_x
            carry[k, 1, at, :] = left_y
        if power:
            acc[...] += total

    def reset():
        for k in range(SUBSTEPS):
            for n in range(2):
                for i in range(nt):
                    carry[k, n, pl.ds(SUB * i, SUB), :] = zero
        acc[...] = zero

    def chunk_in(c):
        return jnp.logical_and(c >= 0, c < nc)

    entries = 2.0 * ns * nz * rows * tiles_c * LANES

    def spread_scale(n, first_sent=None, second_sent=None):
        mine[2 * n] = jnp.sum(acc[...], axis=0, keepdims=True)
        for d in range(1, nz):
            pltpu.make_async_remote_copy(
                src_ref=mine.at[2 * n], dst_ref=red1.at[n, d - 1],
                send_sem=r1_snd.at[n], recv_sem=r1_rcv.at[n],
                device_id={"strip": lax.rem(strip + d, nz)}, device_id_type=MESH,
            ).start()
        if first_sent is not None:
            first_sent()
        wait_bytes(red1.at[n], r1_rcv.at[n])
        mine[2 * n + 1] = mine[2 * n] + jnp.sum(red1[n], axis=0)
        for d in range(ns - 1, 0, -1):
            pltpu.make_async_remote_copy(
                src_ref=mine.at[2 * n + 1], dst_ref=red2.at[n, d - 1],
                send_sem=r2_snd.at[n], recv_sem=r2_rcv.at[n],
                device_id={"sec": lax.rem(sec + d, ns)}, device_id_type=MESH,
            ).start()
        if second_sent is not None:
            second_sent()
        wait_bytes(red2.at[n], r2_rcv.at[n])
        whole = mine[2 * n + 1] + jnp.sum(red2[n], axis=0)
        wait_bytes(red1.at[n], r1_snd.at[n])
        wait_bytes(red2.at[n], r2_snd.at[n])
        power = jnp.sum(whole, axis=1, keepdims=True) * (1.0 / (STEP_SIZE * STEP_SIZE))
        spread = jnp.sqrt(power * (1.0 / entries) + EPSILON)
        scale = jnp.minimum(1.0, SPEED_CAP / spread)
        return jnp.broadcast_to(scale * DAMPING, (SUB, LANES))

    plain = DAMPING

    def wave(w, order, sweep, first_damping, own_rows, final=False, power=True, before=None):
        for k in range(SUBSTEPS):
            c = w - k
            last = k == SUBSTEPS - 1

            @pl.when(chunk_in(c))
            def _():
                if before is not None and k == 1:
                    before(c)
                level(
                    k, c, order[k], order[k + 1], sweep,
                    first_damping if k == 0 else plain,
                    own_rows and last, power and last, final and last,
                )

    def boundary(sweep, c):
        for d in range(2):
            wait_bytes(rx.at[sweep, d, :, pl.ds(c * WIDE, WIDE), pl.ds(0, 2 * SUB)], e_rcv.at[d, c, 0])
        for p in range(2):
            make_target(sweep, c, *pieces[p])
        strip_start(t_halo(sweep, c))

    def interior(sweep, c):
        for d in range(2):
            wait_bytes(
                rx.at[sweep, d, :, pl.ds(c * WIDE, WIDE), pl.ds(SUB, rows - 2 * SUB)], e_rcv.at[d, c, 1]
            )
        make_target(sweep, c, *pieces[2])
        strip_wait_recv(t_halo(sweep, c))

    def sent(sweep):
        def before(c):
            for d in range(2):
                wait_bytes(rx.at[sweep, d, :, pl.ds(c * WIDE, WIDE)], e_snd.at[d, c])

        return before

    reset()
    strip_wait_send(u_halo)
    strip_wait_send(raw_halo)

    def round0(w, _):
        @pl.when(w < nc)
        def _():
            boundary(0, w)

        @pl.when(chunk_in(w - 1))
        def _():
            interior(0, w - 1)

        wave(w - 1, (sa, sb, sa, sb, sa), 0, None, False, before=sent(0))
        return 0

    lax.fori_loop(0, nc + SUBSTEPS, round0, 0)
    damping1 = spread_scale(0)

    reset()
    soon, ahead = min(3, nc), min(4, nc)

    def round1(w, _):
        wave(w, (sa, sb, sa, sb, sc), 0, damping1, True)
        c = w - (SUBSTEPS - 1)

        @pl.when(chunk_in(c))
        def _():
            make_down(1, c, sc)
            strip_start(s_halo(c))

        @pl.when(jnp.logical_and(c >= 0, c < soon))
        def _():
            e_send(1, c, sc)

        return 0

    lax.fori_loop(0, nc + SUBSTEPS - 1, round1, 0)

    def send_next():
        for c in range(soon, ahead):
            e_send(1, c, sc)

    def send_rest():
        def body(c, _):
            e_send(1, c, sc)
            return 0

        def early(c, _):
            boundary(1, c)
            return 0

        lax.fori_loop(ahead, nc, body, 0)
        lax.fori_loop(0, ahead, early, 0)

    damping2 = spread_scale(1, send_next, send_rest)

    reset()
    strip_wait_all(hears_from, sc.at[:, :, top_halo, :], h1_rcv)
    strip_wait_all(sends_to, sc.at[:, :, top_halo, :], h1_snd)

    def round2(w, _):
        @pl.when(jnp.logical_and(w >= ahead, w < nc))
        def _():
            boundary(1, w)

        @pl.when(chunk_in(w - 1))
        def _():
            interior(1, w - 1)

        wave(w - 1, (sc, sb, sc, sb, sc), 1, damping2, False, before=sent(1))
        return 0

    lax.fori_loop(0, nc + SUBSTEPS, round2, 0)
    damping3 = spread_scale(2)

    reset()

    def out_copies(j):
        cols = pl.ds(pl.multiple_of(j * LANES, LANES), LANES)
        return (
            pltpu.make_async_copy(sa.at[0:2, j, own, :], out_u.at[:, 0, :, cols], out_sem.at[0]),
            pltpu.make_async_copy(sa.at[2:4, j, own, :], out_v.at[:, 0, :, cols], out_sem.at[0]),
        )

    def round3(w, _):
        wave(w, (sc, sb, sc, sb, sa), 1, damping3, True, final=True, power=False)
        c = w - (SUBSTEPS - 1)

        @pl.when(chunk_in(c))
        def _():
            for jj in range(WIDE):
                for copy in out_copies(c * WIDE + jj):
                    copy.start()

        return 0

    lax.fori_loop(0, nc + SUBSTEPS - 1, round3, 0)

    for sweep in range(2):
        strip_wait_all(sends_to, tgt.at[sweep, :, :, top_halo, :], th_snd.at[sweep])
    wait_bytes(sa.at[:, :, own, :], out_sem.at[0])


def relax(mesh, start_offsets, section_flow, fixed_nodes, links_across, links_down):
    ns, nz = mesh.shape["sec"], mesh.shape["strip"]
    rows, columns = fixed_nodes.shape[1:]
    tiles_c = columns // LANES
    nc = tiles_c // WIDE
    padded = rows + 2 * HALO
    f32 = jnp.float32
    state = pltpu.VMEM((4, tiles_c, padded + SUB, LANES), f32)
    dma = pltpu.SemaphoreType.DMA
    out = jax.ShapeDtypeStruct(start_offsets.shape, f32)
    return pl.pallas_call(
        functools.partial(kernel, ns, nz, rows, tiles_c),
        out_shape=(out, out),
        in_specs=[pl.BlockSpec(memory_space=pl.ANY)] * 5,
        out_specs=(pl.BlockSpec(memory_space=pl.ANY), pl.BlockSpec(memory_space=pl.ANY)),
        scratch_shapes=[
            state, state, state,
            pltpu.VMEM((2, 2, tiles_c, padded, LANES), f32),
            pltpu.VMEM((3, tiles_c, padded, LANES), f32),
            pltpu.VMEM((3, tiles_c, padded, LANES), jnp.int32),
            pltpu.VMEM((2, tiles_c, rows, LANES), f32),
            pltpu.VMEM((2, 2, tiles_c, rows, LANES), f32),
            pltpu.VMEM((2, 2, 2, tiles_c, rows, LANES), f32),
            pltpu.VMEM((SUBSTEPS, 2, padded, LANES), f32),
            pltpu.VMEM((SUB, LANES), f32),
            pltpu.VMEM((6, 1, LANES), f32),
            pltpu.VMEM((3, nz - 1, 1, LANES), f32),
            pltpu.VMEM((3, ns - 1, 1, LANES), f32),
            dma((nc,)), dma((1,)),
            dma((2, nc)), dma((2, nc, 2)),
            dma((2, 2)), dma((2, nc)),
            dma((2, 2)), dma((2, 2)),
            dma((2,)), dma((2,)),
            dma((3,)), dma((3,)), dma((3,)), dma((3,)),
            dma((1,)),
        ],
        compiler_params=pltpu.CompilerParams(
            collective_id=0, has_side_effects=True, vmem_limit_bytes=60 * 1024 * 1024
        ),
    )(start_offsets, section_flow, fixed_nodes, links_across, links_down)


def solution(mesh):
    whole = P(None, "sec", "strip", None)
    flags = P("sec", "strip", None)
    return jax.shard_map(
        functools.partial(relax, mesh),
        mesh=mesh,
        in_specs=(whole, whole, flags, flags, flags),
        out_specs=(whole, whole),
        check_vma=False,
    )
```

```python
import functools

import jax
import jax.numpy as jnp
from jax import lax
from jax.experimental import pallas as pl
from jax.experimental.pallas import tpu as pltpu
from jax.sharding import PartitionSpec as P

SPRING = 1.0
COUPLING = 0.5
STEP_SIZE = 0.4
DAMPING = 0.9
SPEED_CAP = 0.05
EPSILON = 1e-06
SUBSTEPS = 4

LINK = 0.5 * SPRING * STEP_SIZE * STEP_SIZE
PULL = COUPLING * STEP_SIZE * STEP_SIZE

HALO = 8
SUB = 8
LANES = 128
WIDE = 2
HALF = LANES // 2
MESH = pl.DeviceIdType.MESH


def vreg_iota(axis):
    return lax.broadcasted_iota(jnp.int32, (SUB, LANES), axis)


def pick(x, index):
    return jnp.take_along_axis(x, index, axis=1, mode="promise_in_bounds")


def split_columns(first, second):
    lane = vreg_iota(1)
    low = lane < HALF
    a = pick(first, jnp.where(low, 2 * lane, 2 * lane - (LANES - 1)))
    b = pick(second, jnp.where(low, 2 * lane + 1, 2 * lane - LANES))
    return jnp.where(low, a, b), pltpu.roll(jnp.where(low, b, a), HALF, 1)


def join_columns(even, odd):
    lane = vreg_iota(1)
    low = lane < HALF
    half = lax.shift_right_logical(lane, 1)
    is_even = lax.bitwise_and(lane, 1) == 0
    turned = pltpu.roll(odd, HALF, 1)
    first = pick(jnp.where(low, even, turned), jnp.where(is_even, half, half + HALF))
    second = pick(jnp.where(low, turned, even), jnp.where(is_even, half + HALF, half))
    return first, second


def substeps(rows, tiles_c, coef, carry, acc, hold):
    nc = tiles_c // WIDE
    nt = (rows + 2 * HALO) // SUB
    zero = jnp.zeros((SUB, LANES), jnp.float32)
    lane, sublane = vreg_iota(1), vreg_iota(0)
    first_lane, first_sub = lane == 0, sublane == 0

    def level(k, c, src, dst, tgt, damping, own_rows, power=False, mode="step"):
        lo, hi = (HALO // SUB, nt - HALO // SUB) if own_rows else (0, nt)
        j0 = c * WIDE
        beyond = jnp.minimum(j0 + WIDE, tiles_c - WIDE)
        js = [j0, j0 + 1]
        up_x, up_y = [zero] * WIDE, [zero] * WIDE
        total = zero

        def down_pull(i, jj, ux, uy):
            after = pl.ds(SUB * i + 1, SUB)
            dx = src[0, js[jj], after, :] - ux
            dy = src[1, js[jj], after, :] - uy
            ey = dy + 1.0
            stretch = dx * dx + dy * (ey + 1.0)
            pull = stretch * coef[1, js[jj], pl.ds(SUB * i, SUB), :]
            return pull * dx, pull * ey

        if own_rows:
            at = pl.ds(SUB * (lo - 1), SUB)
            for jj in range(WIDE):
                hx, hy = down_pull(lo - 1, jj, src[0, js[jj], at, :], src[1, js[jj], at, :])
                up_x[jj], up_y[jj] = pltpu.roll(hx, 1, 0), pltpu.roll(hy, 1, 0)
        for i in range(lo, hi):
            at = pl.ds(SUB * i, SUB)
            ux = [src[0, j, at, :] for j in js]
            uy = [src[1, j, at, :] for j in js]
            right_x = (ux[1], pltpu.roll(jnp.where(first_lane, src[0, beyond, at, :], ux[0]), LANES - 1, 1))
            right_y = (uy[1], pltpu.roll(jnp.where(first_lane, src[1, beyond, at, :], uy[0]), LANES - 1, 1))
            pull_x, pull_y = [], []
            for jj in range(WIDE):
                dx, dy = right_x[jj] - ux[jj], right_y[jj] - uy[jj]
                ex = dx + 1.0
                pull = (dx * (ex + 1.0) + dy * dy) * coef[0, js[jj], at, :]
                pull_x.append(pull * ex)
                pull_y.append(pull * dy)
            gx, gy = pltpu.roll(pull_x[1], 1, 1), pltpu.roll(pull_y[1], 1, 1)
            left_x = (jnp.where(first_lane, carry[k, 0, at, :], gx), pull_x[0])
            left_y = (jnp.where(first_lane, carry[k, 1, at, :], gy), pull_y[0])
            carry[k, 0, at, :] = gx
            carry[k, 1, at, :] = gy
            done = []
            for jj in range(WIDE):
                j = js[jj]
                fx = pull_x[jj] - left_x[jj]
                fy = pull_y[jj] - left_y[jj]
                hx, hy = down_pull(i, jj, ux[jj], uy[jj])
                vx, vy = pltpu.roll(hx, 1, 0), pltpu.roll(hy, 1, 0)
                fx = fx + (hx - jnp.where(first_sub, up_x[jj], vx))
                fy = fy + (hy - jnp.where(first_sub, up_y[jj], vy))
                up_x[jj], up_y[jj] = vx, vy
                fx = fx + (tgt[0, j, at, :] - hold * ux[jj])
                fy = fy + (tgt[1, j, at, :] - hold * uy[jj])
                if damping is not None:
                    fx = fx + damping * src[2, j, at, :]
                    fy = fy + damping * src[3, j, at, :]
                if mode == "pre":
                    dst[0, j, at, :] = fx
                    dst[1, j, at, :] = fy
                    continue
                mobility = coef[2, j, at, :]
                wx, wy = mobility * fx, mobility * fy
                new = (ux[jj] + wx, uy[jj] + wy)
                if mode == "final":
                    done.append(new + (wx * (1.0 / STEP_SIZE), wy * (1.0 / STEP_SIZE)))
                else:
                    for n, x in enumerate(new + (wx, wy)):
                        dst[n, j, at, :] = x
                if power and HALO // SUB <= i < nt - HALO // SUB:
                    total = total + (wx * wx + wy * wy)
            if mode == "final":
                for n in range(4):
                    for jj, x in enumerate(join_columns(done[0][n], done[1][n])):
                        dst[n // 2, n % 2, js[jj], pl.ds(SUB * i - HALO, SUB), :] = x
        if power:
            acc[...] += total

    def apply(c, src, pre, dst, damping):
        for i in range(nt):
            at = pl.ds(SUB * i, SUB)
            for jj in range(WIDE):
                j = c * WIDE + jj
                for n in range(2):
                    w = coef[2, j, at, :] * (pre[n, j, at, :] + damping * src[2 + n, j, at, :])
                    dst[n, j, at, :] = src[n, j, at, :] + w
                    dst[2 + n, j, at, :] = w

    return level, apply


def clear_carry(carry, rows):
    zero = jnp.zeros((SUB, LANES), jnp.float32)
    for k in range(SUBSTEPS):
        for n in range(2):
            for i in range((rows + 2 * HALO) // SUB):
                carry[k, n, pl.ds(SUB * i, SUB), :] = zero


def pull_of(sec, ns):
    links = (sec > 0).astype(jnp.float32) + (sec < ns - 1).astype(jnp.float32)
    return jnp.full((SUB, LANES), PULL, jnp.float32) * links


def kernel(
    ns, nz, rows, tiles_c,
    u0, flow, fixed, links_a, links_d, sc, tgt1, coef, pre, damping_out,
    sa, sb, tgt0, raw, fl, sd, rx, carry, acc, mine, red1, red2,
    ld_s, ld_g, e_snd, e_rcv, th_snd, th_rcv, h0_snd, h0_rcv, h1_snd, h1_rcv,
    r1_snd, r1_rcv, r2_snd, r2_rcv,
):
    nc = tiles_c // WIDE
    nt = (rows + 2 * HALO) // SUB
    sec = lax.axis_index("sec")
    strip = lax.axis_index("strip")
    sec_up, sec_dn = lax.rem(sec + 1, ns), lax.rem(sec + ns - 1, ns)
    has_above_strip, has_below_strip = strip > 0, strip < nz - 1
    own = pl.ds(HALO, rows)
    tgt = (tgt0, tgt1)

    def wait_bytes(ref, sem):
        pltpu.make_async_copy(ref, ref, sem).wait()

    def start_u(j, _):
        cols = pl.ds(pl.multiple_of(j * LANES, LANES), LANES)
        sem = ld_s.at[j // WIDE]
        pltpu.make_async_copy(u0.at[:, 0, :, cols], sb.at[0:2, j, own, :], sem).start()
        pltpu.make_async_copy(flow.at[:, 0, :, cols], sb.at[2:4, j, own, :], sem).start()
        return 0

    def start_g(j, _):
        cols = pl.ds(pl.multiple_of(j * LANES, LANES), LANES)
        for n, ref in enumerate((links_a, links_d, fixed)):
            pltpu.make_async_copy(ref.at[0, :, cols], raw.at[n, j, own, :], ld_g.at[0]).start()
        return 0

    lax.fori_loop(0, tiles_c, start_u, 0)
    lax.fori_loop(0, tiles_c, start_g, 0)

    barrier = pltpu.get_barrier_semaphore()

    def greet_strip(d, _):
        pl.semaphore_signal(barrier, inc=1, device_id={"strip": lax.rem(strip + d, nz)}, device_id_type=MESH)
        return 0

    def greet_sec(d, _):
        pl.semaphore_signal(barrier, inc=1, device_id={"sec": lax.rem(sec + d, ns)}, device_id_type=MESH)
        return 0

    lax.fori_loop(1, nz, greet_strip, 0)
    lax.fori_loop(1, ns, greet_sec, 0)

    zero = jnp.zeros((SUB, LANES), jnp.float32)
    zero_i = jnp.zeros((SUB, LANES), jnp.int32)

    def clear(at):
        def body(j, _):
            for n in range(3):
                raw[n, j, at, :] = zero_i
            for n in range(2):
                sa[n, j, at, :] = zero
                tgt0[n, j, at, :] = zero
                tgt1[n, j, at, :] = zero
            for n in range(4):
                sc[n, j, at, :] = zero
            return 0

        lax.fori_loop(0, tiles_c, body, 0)

    top_halo, bottom_halo = pl.ds(0, HALO), pl.ds(HALO + rows, HALO)
    top_own, bottom_own = pl.ds(HALO, HALO), pl.ds(rows, HALO)

    @pl.when(jnp.logical_not(has_above_strip))
    def _():
        clear(top_halo)

    @pl.when(jnp.logical_not(has_below_strip))
    def _():
        clear(bottom_halo)

    pieces = ((0, SUB), (rows - SUB, SUB), (SUB, rows - 2 * SUB))

    def e_copy(sweep, d, c, p, state):
        first, count = pieces[p]
        chunk = pl.ds(c * WIDE, WIDE)
        if d == 0:
            src = state.at[0:2, chunk, pl.ds(HALO + first, count), :]
        else:
            src = sd.at[sweep, :, chunk, pl.ds(first, count), :]
        return pltpu.make_async_remote_copy(
            src_ref=src,
            dst_ref=rx.at[sweep, d, :, chunk, pl.ds(first, count), :],
            send_sem=e_snd.at[d, c],
            recv_sem=e_rcv.at[d, c, p // 2],
            device_id={"sec": sec_up if d == 0 else sec_dn},
            device_id_type=MESH,
        )

    def strip_copy(ref_of, d, snd, rcv):
        return pltpu.make_async_remote_copy(
            src_ref=ref_of(top_own if d == 0 else bottom_own),
            dst_ref=ref_of(bottom_halo if d == 0 else top_halo),
            send_sem=snd,
            recv_sem=rcv,
            device_id={"strip": strip + (-1 if d == 0 else 1)},
            device_id_type=MESH,
        )

    sends_to = (has_above_strip, has_below_strip)
    hears_from = (has_below_strip, has_above_strip)

    def strip_start(make):
        for d in range(2):
            @pl.when(sends_to[d])
            def _():
                make(d).start()

    def strip_wait_send(make):
        for d in range(2):
            @pl.when(sends_to[d])
            def _():
                make(d).wait_send()

    def strip_wait_recv(make):
        for d in range(2):
            @pl.when(hears_from[d])
            def _():
                make(d).wait_recv()

    def t_halo(sweep, c):
        chunk = pl.ds(c * WIDE, WIDE)
        return lambda d: strip_copy(
            lambda at: tgt[sweep].at[:, chunk, at, :], d, th_snd.at[sweep, d], th_rcv.at[d, c]
        )

    def u_halo(d):
        return strip_copy(lambda at: sa.at[0:2, :, at, :], d, h0_snd.at[0, d], h0_rcv.at[0, d])

    def raw_halo(d):
        return strip_copy(lambda at: raw.at[:, :, at, :], d, h0_snd.at[1, d], h0_rcv.at[1, d])

    def s_halo(c):
        chunk = pl.ds(c * WIDE, WIDE)
        return lambda d: strip_copy(
            lambda at: sc.at[:, chunk, at, :], d, h1_snd.at[d], h1_rcv.at[d]
        )

    def strip_wait_all(on, ref, sem):
        for d in range(2):
            @pl.when(on[d])
            def _():
                wait_bytes(ref, sem.at[d])

    def make_down(sweep, c, state):
        for jj in range(WIDE):
            j = c * WIDE + jj
            for n in range(2):
                sd[sweep, n, j] = state[n, j, own, :] - fl[n, j]

    def e_send(sweep, c, state):
        for d in range(2):
            for p in range(3):
                e_copy(sweep, d, c, p, state).start()

    def prepare(c):
        wait_bytes(rx.at[0, :, :, pl.ds(c * WIDE, WIDE)], ld_s.at[c])
        j = c * WIDE
        for i in range(rows // SUB):
            wide, at = pl.ds(HALO + SUB * i, SUB), pl.ds(SUB * i, SUB)
            for n in range(2):
                u = split_columns(sb[n, j, wide, :], sb[n, j + 1, wide, :])
                f = split_columns(sb[2 + n, j, wide, :], sb[2 + n, j + 1, wide, :])
                for jj in range(WIDE):
                    sa[n, j + jj, wide, :] = u[jj]
                    fl[n, j + jj, at, :] = f[jj]
                    sd[0, n, j + jj, at, :] = u[jj] - f[jj]

    def first_sends(c, _):
        prepare(c)
        e_send(0, c, sa)
        return 0

    prepare(0)
    pl.semaphore_wait(barrier, nz - 1 + ns - 1)
    e_send(0, 0, sa)
    lax.fori_loop(1, nc, first_sends, 0)
    strip_start(u_halo)

    wait_bytes(raw.at[:, :, own, :], ld_g.at[0])
    strip_start(raw_halo)
    strip_wait_recv(u_halo)
    strip_wait_recv(raw_halo)

    lane, sublane = vreg_iota(1), vreg_iota(0)
    first_lane, last_lane = lane == 0, lane == LANES - 1
    first_sub = sublane == 0

    def convert(c, _):
        j = c * WIDE
        edge = jnp.logical_and(last_lane, c == nc - 1)
        for i in range(nt):
            at = pl.ds(SUB * i, SUB)
            for n in range(3):
                parts = split_columns(
                    raw[n, j, at, :].astype(jnp.float32), raw[n, j + 1, at, :].astype(jnp.float32)
                )
                for jj in range(WIDE):
                    x = 1.0 - parts[jj] if n == 2 else parts[jj] * LINK
                    if n == 0 and jj == 1:
                        x = jnp.where(edge, 0.0, x)
                    if n == 1 and SUB * i == rows:
                        bottom = jnp.logical_and(sublane == SUB - 1, strip == nz - 1)
                        x = jnp.where(bottom, 0.0, x)
                    coef[n, j + jj, at, :] = x
        return 0

    lax.fori_loop(0, nc, convert, 0)

    has_below, has_above = sec > 0, sec < ns - 1
    hold = pull_of(sec, ns)
    below_on = jnp.broadcast_to(has_below, (SUB, LANES))
    above_on = jnp.broadcast_to(has_above, (SUB, LANES))

    def make_target(sweep, c, first, count):
        for jj in range(WIDE):
            j = c * WIDE + jj
            for i in range(first // SUB, (first + count) // SUB):
                at = pl.ds(SUB * i, SUB)
                for n in range(2):
                    below = jnp.where(below_on, rx[sweep, 0, n, j, at, :] + fl[n, j, at, :], 0.0)
                    above = jnp.where(above_on, rx[sweep, 1, n, j, at, :], 0.0)
                    tgt[sweep][n, j, pl.ds(HALO + SUB * i, SUB), :] = (below + above) * PULL

    level, apply = substeps(rows, tiles_c, coef, carry, acc, hold)

    def reset():
        clear_carry(carry, rows)
        acc[...] = zero

    def forces(src, sweep):
        def body(c, _):
            level(0, c, src, pre, tgt[sweep], None, False, mode="pre")
            return 0

        reset()
        lax.fori_loop(0, nc, body, 0)

    def chunk_in(c):
        return jnp.logical_and(c >= 0, c < nc)

    entries = 2.0 * ns * nz * rows * tiles_c * LANES

    def spread_scale(n, first_sent=None, second_sent=None):
        mine[2 * n] = jnp.sum(acc[...], axis=0, keepdims=True)
        for d in range(1, nz):
            pltpu.make_async_remote_copy(
                src_ref=mine.at[2 * n], dst_ref=red1.at[n, d - 1],
                send_sem=r1_snd.at[n], recv_sem=r1_rcv.at[n],
                device_id={"strip": lax.rem(strip + d, nz)}, device_id_type=MESH,
            ).start()
        if first_sent is not None:
            first_sent()
        wait_bytes(red1.at[n], r1_rcv.at[n])
        mine[2 * n + 1] = mine[2 * n] + jnp.sum(red1[n], axis=0)
        for d in range(ns - 1, 0, -1):
            pltpu.make_async_remote_copy(
                src_ref=mine.at[2 * n + 1], dst_ref=red2.at[n, d - 1],
                send_sem=r2_snd.at[n], recv_sem=r2_rcv.at[n],
                device_id={"sec": lax.rem(sec + d, ns)}, device_id_type=MESH,
            ).start()
        if second_sent is not None:
            second_sent()
        wait_bytes(red2.at[n], r2_rcv.at[n])
        whole = mine[2 * n + 1] + jnp.sum(red2[n], axis=0)
        wait_bytes(red1.at[n], r1_snd.at[n])
        wait_bytes(red2.at[n], r2_snd.at[n])
        power = jnp.sum(whole, axis=1, keepdims=True) * (1.0 / (STEP_SIZE * STEP_SIZE))
        spread = jnp.sqrt(power * (1.0 / entries) + EPSILON)
        scale = jnp.minimum(1.0, SPEED_CAP / spread)
        return jnp.broadcast_to(scale * DAMPING, (SUB, LANES))

    plain = DAMPING

    def wave(w, order, sweep, first_damping, own_rows, before=None, known=False):
        for k in range(SUBSTEPS):
            c = w - k
            last = k == SUBSTEPS - 1

            @pl.when(chunk_in(c))
            def _():
                if before is not None and k == 1:
                    before(c)
                if known and k == 0:
                    apply(c, order[0], pre, order[1], first_damping)
                else:
                    level(
                        k, c, order[k], order[k + 1], tgt[sweep],
                        first_damping if k == 0 else plain, own_rows and last, last,
                    )

    def boundary(sweep, c):
        for d in range(2):
            wait_bytes(rx.at[sweep, d, :, pl.ds(c * WIDE, WIDE), pl.ds(0, 2 * SUB)], e_rcv.at[d, c, 0])
        for p in range(2):
            make_target(sweep, c, *pieces[p])
        strip_start(t_halo(sweep, c))

    def interior(sweep, c):
        for d in range(2):
            wait_bytes(
                rx.at[sweep, d, :, pl.ds(c * WIDE, WIDE), pl.ds(SUB, rows - 2 * SUB)], e_rcv.at[d, c, 1]
            )
        make_target(sweep, c, *pieces[2])
        strip_wait_recv(t_halo(sweep, c))

    def sent(sweep):
        def before(c):
            for d in range(2):
                wait_bytes(rx.at[sweep, d, :, pl.ds(c * WIDE, WIDE)], e_snd.at[d, c])

        return before

    reset()
    strip_wait_send(u_halo)
    strip_wait_send(raw_halo)

    def round0(w, _):
        @pl.when(w < nc)
        def _():
            boundary(0, w)

        @pl.when(chunk_in(w - 1))
        def _():
            interior(0, w - 1)

        wave(w - 1, (sa, sb, sa, sb, sa), 0, None, False, before=sent(0))
        return 0

    lax.fori_loop(0, nc + SUBSTEPS, round0, 0)
    damping1 = spread_scale(0, lambda: forces(sa, 0))

    soon, ahead = min(3, nc), min(4, nc)

    def round1(w, _):
        wave(w, (sa, sb, sa, sb, sc), 0, damping1, True, known=True)
        c = w - (SUBSTEPS - 1)

        @pl.when(chunk_in(c))
        def _():
            make_down(1, c, sc)
            strip_start(s_halo(c))

        @pl.when(jnp.logical_and(c >= 0, c < soon))
        def _():
            e_send(1, c, sc)

        return 0

    lax.fori_loop(0, nc + SUBSTEPS - 1, round1, 0)

    def send_next():
        for c in range(soon, ahead):
            e_send(1, c, sc)

    def send_rest():
        def body(c, _):
            e_send(1, c, sc)
            return 0

        def early(c, _):
            boundary(1, c)
            return 0

        lax.fori_loop(ahead, nc, body, 0)
        lax.fori_loop(0, ahead, early, 0)

    damping2 = spread_scale(1, send_next, send_rest)

    reset()
    strip_wait_all(hears_from, sc.at[:, :, top_halo, :], h1_rcv)
    strip_wait_all(sends_to, sc.at[:, :, top_halo, :], h1_snd)

    def round2(w, _):
        @pl.when(jnp.logical_and(w >= ahead, w < nc))
        def _():
            boundary(1, w)

        @pl.when(chunk_in(w - 1))
        def _():
            interior(1, w - 1)

        wave(w - 1, (sc, sb, sc, sb, sc), 1, damping2, False, before=sent(1))
        return 0

    lax.fori_loop(0, nc + SUBSTEPS, round2, 0)
    damping_out[...] = spread_scale(2, lambda: forces(sc, 1))
    for sweep in range(2):
        strip_wait_all(sends_to, tgt[sweep].at[:, :, top_halo, :], th_snd.at[sweep])


def last_round(
    ns, rows, tiles_c,
    state, tgt, coef, pre, damping, out_u, out_v,
    sa, sb, stage, carry, out_sem,
):
    nc = tiles_c // WIDE
    level, apply = substeps(rows, tiles_c, coef, carry, None, pull_of(lax.axis_index("sec"), ns))
    clear_carry(carry, rows)
    first = damping[...]

    def wave(w, _):
        for k in range(SUBSTEPS):
            c = w - k

            @pl.when(jnp.logical_and(c >= 0, c < nc))
            def _():
                if k == 0:
                    apply(c, state, pre, sb, first)
                elif k == 1:
                    level(k, c, sb, sa, tgt, DAMPING, False)
                elif k == 2:
                    level(k, c, sa, sb, tgt, DAMPING, False)
                else:
                    level(k, c, sb, stage, tgt, DAMPING, True, mode="final")
                    for jj in range(WIDE):
                        j = c * WIDE + jj
                        cols = pl.ds(pl.multiple_of(j * LANES, LANES), LANES)
                        for n, out in enumerate((out_u, out_v)):
                            pltpu.make_async_copy(
                                stage.at[n, :, j], out.at[:, 0, :, cols], out_sem.at[0]
                            ).start()

        return 0

    lax.fori_loop(0, nc + SUBSTEPS - 1, wave, 0)
    pltpu.make_async_copy(stage, stage, out_sem.at[0]).wait()


def relax(mesh, start_offsets, section_flow, fixed_nodes, links_across, links_down):
    ns, nz = mesh.shape["sec"], mesh.shape["strip"]
    rows, columns = fixed_nodes.shape[1:]
    tiles_c = columns // LANES
    nc = tiles_c // WIDE
    padded = rows + 2 * HALO
    f32 = jnp.float32
    state = (4, tiles_c, padded + SUB, LANES)
    planes = lambda n: (n, tiles_c, padded, LANES)
    lines = pltpu.VMEM((SUBSTEPS, 2, padded, LANES), f32)
    dma = pltpu.SemaphoreType.DMA
    anywhere = pl.BlockSpec(memory_space=pltpu.HBM)
    near = pl.BlockSpec(memory_space=pltpu.VMEM)
    handed = (state, planes(2), planes(3), planes(2), (SUB, LANES))
    between = pl.pallas_call(
        functools.partial(kernel, ns, nz, rows, tiles_c),
        out_shape=tuple(pltpu.VMEM(shape, f32) for shape in handed),
        in_specs=[anywhere] * 5,
        out_specs=(near,) * len(handed),
        scratch_shapes=[
            pltpu.VMEM(state, f32),
            pltpu.VMEM(state, f32),
            pltpu.VMEM(planes(2), f32),
            pltpu.VMEM(planes(3), jnp.int32),
            pltpu.VMEM((2, tiles_c, rows, LANES), f32),
            pltpu.VMEM((2, 2, tiles_c, rows, LANES), f32),
            pltpu.VMEM((2, 2, 2, tiles_c, rows, LANES), f32),
            lines,
            pltpu.VMEM((SUB, LANES), f32),
            pltpu.VMEM((6, 1, LANES), f32),
            pltpu.VMEM((3, nz - 1, 1, LANES), f32),
            pltpu.VMEM((3, ns - 1, 1, LANES), f32),
            dma((nc,)), dma((1,)),
            dma((2, nc)), dma((2, nc, 2)),
            dma((2, 2)), dma((2, nc)),
            dma((2, 2)), dma((2, 2)),
            dma((2,)), dma((2,)),
            dma((3,)), dma((3,)), dma((3,)), dma((3,)),
        ],
        compiler_params=pltpu.CompilerParams(
            collective_id=0, has_side_effects=True, vmem_limit_bytes=107 * 512 * 1024
        ),
    )(start_offsets, section_flow, fixed_nodes, links_across, links_down)
    between = [pltpu.with_memory_space_constraint(x, pltpu.VMEM) for x in between]
    out = jax.ShapeDtypeStruct(start_offsets.shape, f32)
    return pl.pallas_call(
        functools.partial(last_round, ns, rows, tiles_c),
        out_shape=(out, out),
        in_specs=[near] * len(handed),
        out_specs=(anywhere, anywhere),
        scratch_shapes=[
            pltpu.VMEM(state, f32),
            pltpu.VMEM(state, f32),
            pltpu.VMEM((2, 2, tiles_c, rows, LANES), f32),
            lines,
            dma((1,)),
        ],
        compiler_params=pltpu.CompilerParams(
            vmem_limit_bytes=24 * 1024 * 1024
        ),
    )(*between)


def solution(mesh):
    whole = P(None, "sec", "strip", None)
    flags = P("sec", "strip", None)
    return jax.shard_map(
        functools.partial(relax, mesh),
        mesh=mesh,
        in_specs=(whole, whole, flags, flags, flags),
        out_specs=(whole, whole),
        check_vma=False,
    )
```

```python
import functools

import jax
import jax.numpy as jnp
from jax import lax
from jax.experimental import pallas as pl
from jax.experimental.pallas import tpu as pltpu
from jax.sharding import PartitionSpec as P

SPRING = 1.0
COUPLING = 0.5
STEP_SIZE = 0.4
DAMPING = 0.9
SPEED_CAP = 0.05
EPSILON = 1e-06
SUBSTEPS = 4

LINK = 0.5 * SPRING * STEP_SIZE * STEP_SIZE
PULL = COUPLING * STEP_SIZE * STEP_SIZE

HALO = 8
SUB = 8
LANES = 128
WIDE = 2
HALF = LANES // 2
MESH = pl.DeviceIdType.MESH


def wrap(x, n):
    return jnp.where(x >= n, x - n, x)


def vreg_iota(axis):
    return lax.broadcasted_iota(jnp.int32, (SUB, LANES), axis)


def pick(x, index):
    return jnp.take_along_axis(x, index, axis=1, mode="promise_in_bounds")


def split_columns(first, second):
    lane = vreg_iota(1)
    low = lane < HALF
    a = pick(first, jnp.where(low, 2 * lane, 2 * lane - (LANES - 1)))
    b = pick(second, jnp.where(low, 2 * lane + 1, 2 * lane - LANES))
    return jnp.where(low, a, b), pltpu.roll(jnp.where(low, b, a), HALF, 1)


def join_columns(even, odd):
    lane = vreg_iota(1)
    low = lane < HALF
    half = lax.shift_right_logical(lane, 1)
    is_even = lax.bitwise_and(lane, 1) == 0
    turned = pltpu.roll(odd, HALF, 1)
    first = pick(jnp.where(low, even, turned), jnp.where(is_even, half, half + HALF))
    second = pick(jnp.where(low, turned, even), jnp.where(is_even, half + HALF, half))
    return first, second


def substeps(rows, tiles_c, coef, carry, acc, hold):
    nc = tiles_c // WIDE
    nt = (rows + 2 * HALO) // SUB
    zero = jnp.zeros((SUB, LANES), jnp.float32)
    lane, sublane = vreg_iota(1), vreg_iota(0)
    first_lane, first_sub = lane == 0, sublane == 0

    def level(k, c, src, dst, tgt, damping, own_rows, power=False, mode="step"):
        lo, hi = (HALO // SUB, nt - HALO // SUB) if own_rows else (0, nt)
        j0 = c * WIDE
        beyond = jnp.minimum(j0 + WIDE, tiles_c - WIDE)
        js = [j0, j0 + 1]
        up_x, up_y = [zero] * WIDE, [zero] * WIDE
        total = zero

        def down_pull(i, jj, ux, uy):
            after = pl.ds(SUB * i + 1, SUB)
            dx = src[0, js[jj], after, :] - ux
            dy = src[1, js[jj], after, :] - uy
            ey = dy + 1.0
            stretch = dx * dx + dy * (ey + 1.0)
            pull = stretch * coef[1, js[jj], pl.ds(SUB * i, SUB), :]
            return pull * dx, pull * ey

        if own_rows:
            at = pl.ds(SUB * (lo - 1), SUB)
            for jj in range(WIDE):
                hx, hy = down_pull(lo - 1, jj, src[0, js[jj], at, :], src[1, js[jj], at, :])
                up_x[jj], up_y[jj] = pltpu.roll(hx, 1, 0), pltpu.roll(hy, 1, 0)
        for i in range(lo, hi):
            at = pl.ds(SUB * i, SUB)
            ux = [src[0, j, at, :] for j in js]
            uy = [src[1, j, at, :] for j in js]
            right_x = (ux[1], pltpu.roll(jnp.where(first_lane, src[0, beyond, at, :], ux[0]), LANES - 1, 1))
            right_y = (uy[1], pltpu.roll(jnp.where(first_lane, src[1, beyond, at, :], uy[0]), LANES - 1, 1))
            pull_x, pull_y = [], []
            for jj in range(WIDE):
                dx, dy = right_x[jj] - ux[jj], right_y[jj] - uy[jj]
                ex = dx + 1.0
                pull = (dx * (ex + 1.0) + dy * dy) * coef[0, js[jj], at, :]
                pull_x.append(pull * ex)
                pull_y.append(pull * dy)
            gx, gy = pltpu.roll(pull_x[1], 1, 1), pltpu.roll(pull_y[1], 1, 1)
            left_x = (jnp.where(first_lane, carry[k, 0, at, :], gx), pull_x[0])
            left_y = (jnp.where(first_lane, carry[k, 1, at, :], gy), pull_y[0])
            carry[k, 0, at, :] = gx
            carry[k, 1, at, :] = gy
            done = []
            for jj in range(WIDE):
                j = js[jj]
                fx = pull_x[jj] - left_x[jj]
                fy = pull_y[jj] - left_y[jj]
                hx, hy = down_pull(i, jj, ux[jj], uy[jj])
                vx, vy = pltpu.roll(hx, 1, 0), pltpu.roll(hy, 1, 0)
                fx = fx + (hx - jnp.where(first_sub, up_x[jj], vx))
                fy = fy + (hy - jnp.where(first_sub, up_y[jj], vy))
                up_x[jj], up_y[jj] = vx, vy
                fx = fx + (tgt[0, j, at, :] - hold * ux[jj])
                fy = fy + (tgt[1, j, at, :] - hold * uy[jj])
                if damping is not None:
                    fx = fx + damping * src[2, j, at, :]
                    fy = fy + damping * src[3, j, at, :]
                if mode == "pre":
                    dst[0, j, at, :] = fx
                    dst[1, j, at, :] = fy
                    continue
                mobility = coef[2, j, at, :]
                wx, wy = mobility * fx, mobility * fy
                new = (ux[jj] + wx, uy[jj] + wy)
                if mode == "final":
                    done.append(new + (wx * (1.0 / STEP_SIZE), wy * (1.0 / STEP_SIZE)))
                else:
                    for n, x in enumerate(new + (wx, wy)):
                        dst[n, j, at, :] = x
                if power and HALO // SUB <= i < nt - HALO // SUB:
                    total = total + (wx * wx + wy * wy)
            if mode == "final":
                for n in range(4):
                    for jj, x in enumerate(join_columns(done[0][n], done[1][n])):
                        dst[n // 2, n % 2, js[jj], pl.ds(SUB * i - HALO, SUB), :] = x
        if power:
            acc[...] += total

    def apply(c, src, pre, dst, damping):
        for i in range(nt):
            at = pl.ds(SUB * i, SUB)
            for jj in range(WIDE):
                j = c * WIDE + jj
                for n in range(2):
                    w = coef[2, j, at, :] * (pre[n, j, at, :] + damping * src[2 + n, j, at, :])
                    dst[n, j, at, :] = src[n, j, at, :] + w
                    dst[2 + n, j, at, :] = w

    return level, apply


def clear_carry(carry, rows):
    zero = jnp.zeros((SUB, LANES), jnp.float32)
    for k in range(SUBSTEPS):
        for n in range(2):
            for i in range((rows + 2 * HALO) // SUB):
                carry[k, n, pl.ds(SUB * i, SUB), :] = zero


def pull_of(sec, ns):
    links = (sec > 0).astype(jnp.float32) + (sec < ns - 1).astype(jnp.float32)
    return jnp.full((SUB, LANES), PULL, jnp.float32) * links


def kernel(
    ns, nz, rows, tiles_c,
    u0, flow, fixed, links_a, links_d, sc, tgt1, coef, pre, damping_out,
    sa, sb, tgt0, raw, fl, sd, rx, carry, acc, mine, red1, red2,
    ld_s, ld_g, e_snd, e_rcv, th_snd, th_rcv, h0_snd, h0_rcv, h1_snd, h1_rcv,
    r1_snd, r1_rcv, r2_snd, r2_rcv,
):
    nc = tiles_c // WIDE
    nt = (rows + 2 * HALO) // SUB
    sec = lax.axis_index("sec")
    strip = lax.axis_index("strip")
    sec_up, sec_dn = wrap(sec + 1, ns), wrap(sec + ns - 1, ns)
    has_above_strip, has_below_strip = strip > 0, strip < nz - 1
    own = pl.ds(HALO, rows)
    tgt = (tgt0, tgt1)

    def wait_bytes(ref, sem):
        pltpu.make_async_copy(ref, ref, sem).wait()

    barrier = pltpu.get_barrier_semaphore()
    for d in range(ns - 1, 0, -1):
        pl.semaphore_signal(barrier, inc=1, device_id={"sec": wrap(sec + d, ns)}, device_id_type=MESH)
    for d in range(nz - 1, 0, -1):
        pl.semaphore_signal(barrier, inc=1, device_id={"strip": wrap(strip + d, nz)}, device_id_type=MESH)

    def start_u(c, _):
        for jj in range(WIDE):
            j = c * WIDE + jj
            cols = pl.ds(pl.multiple_of(j * LANES, LANES), LANES)
            pltpu.make_async_copy(u0.at[:, 0, :, cols], sb.at[0:2, j, own, :], ld_s.at[c]).start()
            pltpu.make_async_copy(flow.at[:, 0, :, cols], sb.at[2:4, j, own, :], ld_s.at[c]).start()
        return 0

    def start_g(j, _):
        cols = pl.ds(pl.multiple_of(j * LANES, LANES), LANES)
        for n, ref in enumerate((links_a, links_d, fixed)):
            pltpu.make_async_copy(ref.at[0, :, cols], raw.at[n, j, own, :], ld_g.at[0]).start()
        return 0

    lax.fori_loop(0, nc, start_u, 0)

    zero = jnp.zeros((SUB, LANES), jnp.float32)
    zero_i = jnp.zeros((SUB, LANES), jnp.int32)

    def clear(at):
        def body(j, _):
            for n in range(3):
                raw[n, j, at, :] = zero_i
            for n in range(2):
                sa[n, j, at, :] = zero
                tgt0[n, j, at, :] = zero
                tgt1[n, j, at, :] = zero
            for n in range(4):
                sc[n, j, at, :] = zero
            return 0

        lax.fori_loop(0, tiles_c, body, 0)

    top_halo, bottom_halo = pl.ds(0, HALO), pl.ds(HALO + rows, HALO)
    top_own, bottom_own = pl.ds(HALO, HALO), pl.ds(rows, HALO)

    @pl.when(jnp.logical_not(has_above_strip))
    def _():
        clear(top_halo)

    @pl.when(jnp.logical_not(has_below_strip))
    def _():
        clear(bottom_halo)

    pieces = ((0, SUB), (rows - SUB, SUB), (SUB, rows - 2 * SUB))

    def e_copy(sweep, d, c, p, state):
        first, count = pieces[p]
        chunk = pl.ds(c * WIDE, WIDE)
        if d == 0:
            src = state.at[0:2, chunk, pl.ds(HALO + first, count), :]
        else:
            src = sd.at[sweep, :, chunk, pl.ds(first, count), :]
        return pltpu.make_async_remote_copy(
            src_ref=src,
            dst_ref=rx.at[sweep, d, :, chunk, pl.ds(first, count), :],
            send_sem=e_snd.at[d, c],
            recv_sem=e_rcv.at[d, c, p // 2],
            device_id={"sec": sec_up if d == 0 else sec_dn},
            device_id_type=MESH,
        )

    def strip_copy(ref_of, d, snd, rcv):
        return pltpu.make_async_remote_copy(
            src_ref=ref_of(top_own if d == 0 else bottom_own),
            dst_ref=ref_of(bottom_halo if d == 0 else top_halo),
            send_sem=snd,
            recv_sem=rcv,
            device_id={"strip": strip + (-1 if d == 0 else 1)},
            device_id_type=MESH,
        )

    sends_to = (has_above_strip, has_below_strip)
    hears_from = (has_below_strip, has_above_strip)

    def strip_start(make):
        for d in range(2):
            @pl.when(sends_to[d])
            def _():
                make(d).start()

    def strip_wait_send(make):
        for d in range(2):
            @pl.when(sends_to[d])
            def _():
                make(d).wait_send()

    def strip_wait_recv(make):
        for d in range(2):
            @pl.when(hears_from[d])
            def _():
                make(d).wait_recv()

    def t_halo(sweep, c):
        chunk = pl.ds(c * WIDE, WIDE)
        return lambda d: strip_copy(
            lambda at: tgt[sweep].at[:, chunk, at, :], d, th_snd.at[sweep, d], th_rcv.at[d, c]
        )

    def u_halo(d):
        return strip_copy(lambda at: sa.at[0:2, :, at, :], d, h0_snd.at[0, d], h0_rcv.at[0, d])

    def raw_halo(d):
        return strip_copy(lambda at: raw.at[:, :, at, :], d, h0_snd.at[1, d], h0_rcv.at[1, d])

    def s_halo(c):
        chunk = pl.ds(c * WIDE, WIDE)
        return lambda d: strip_copy(
            lambda at: sc.at[:, chunk, at, :], d, h1_snd.at[d], h1_rcv.at[d]
        )

    def strip_wait_all(on, ref, sem):
        for d in range(2):
            @pl.when(on[d])
            def _():
                wait_bytes(ref, sem.at[d])

    def make_down(sweep, c, state):
        for jj in range(WIDE):
            j = c * WIDE + jj
            for n in range(2):
                sd[sweep, n, j] = state[n, j, own, :] - fl[n, j]

    def e_send(sweep, c, state):
        for d in range(2):
            for p in range(3):
                e_copy(sweep, d, c, p, state).start()

    def prepare(c):
        wait_bytes(rx.at[0, :, :, pl.ds(c * WIDE, WIDE)], ld_s.at[c])
        j = c * WIDE
        for i in range(rows // SUB):
            wide, at = pl.ds(HALO + SUB * i, SUB), pl.ds(SUB * i, SUB)
            for n in range(2):
                u = split_columns(sb[n, j, wide, :], sb[n, j + 1, wide, :])
                f = split_columns(sb[2 + n, j, wide, :], sb[2 + n, j + 1, wide, :])
                for jj in range(WIDE):
                    sa[n, j + jj, wide, :] = u[jj]
                    fl[n, j + jj, at, :] = f[jj]
                    sd[0, n, j + jj, at, :] = u[jj] - f[jj]

    def first_sends(c, _):
        prepare(c)
        e_send(0, c, sa)
        return 0

    prepare(0)
    pl.semaphore_wait(barrier, nz - 1 + ns - 1)
    e_send(0, 0, sa)
    lax.fori_loop(0, tiles_c, start_g, 0)
    lax.fori_loop(1, nc, first_sends, 0)
    strip_start(u_halo)

    wait_bytes(raw.at[:, :, own, :], ld_g.at[0])
    strip_start(raw_halo)
    strip_wait_recv(u_halo)
    strip_wait_recv(raw_halo)

    lane, sublane = vreg_iota(1), vreg_iota(0)
    first_lane, last_lane = lane == 0, lane == LANES - 1
    first_sub = sublane == 0

    def convert(c, _):
        j = c * WIDE
        edge = jnp.logical_and(last_lane, c == nc - 1)
        for i in range(nt):
            at = pl.ds(SUB * i, SUB)
            for n in range(3):
                parts = split_columns(
                    raw[n, j, at, :].astype(jnp.float32), raw[n, j + 1, at, :].astype(jnp.float32)
                )
                for jj in range(WIDE):
                    x = 1.0 - parts[jj] if n == 2 else parts[jj] * LINK
                    if n == 0 and jj == 1:
                        x = jnp.where(edge, 0.0, x)
                    if n == 1 and SUB * i == rows:
                        bottom = jnp.logical_and(sublane == SUB - 1, strip == nz - 1)
                        x = jnp.where(bottom, 0.0, x)
                    coef[n, j + jj, at, :] = x
        return 0

    lax.fori_loop(0, nc, convert, 0)

    has_below, has_above = sec > 0, sec < ns - 1
    hold = pull_of(sec, ns)
    below_on = jnp.broadcast_to(has_below, (SUB, LANES))
    above_on = jnp.broadcast_to(has_above, (SUB, LANES))

    def make_target(sweep, c, first, count):
        for jj in range(WIDE):
            j = c * WIDE + jj
            for i in range(first // SUB, (first + count) // SUB):
                at = pl.ds(SUB * i, SUB)
                for n in range(2):
                    below = jnp.where(below_on, rx[sweep, 0, n, j, at, :] + fl[n, j, at, :], 0.0)
                    above = jnp.where(above_on, rx[sweep, 1, n, j, at, :], 0.0)
                    tgt[sweep][n, j, pl.ds(HALO + SUB * i, SUB), :] = (below + above) * PULL

    level, apply = substeps(rows, tiles_c, coef, carry, acc, hold)

    def reset():
        clear_carry(carry, rows)
        acc[...] = zero

    def forces(src, sweep):
        def body(c, _):
            level(0, c, src, pre, tgt[sweep], None, False, mode="pre")
            return 0

        reset()
        lax.fori_loop(0, nc, body, 0)

    def chunk_in(c):
        return jnp.logical_and(c >= 0, c < nc)

    entries = 2.0 * ns * nz * rows * tiles_c * LANES

    def spread_scale(n, first_sent=None, second_sent=None):
        mine[2 * n] = jnp.sum(acc[...], axis=0, keepdims=True)
        for d in range(1, nz):
            pltpu.make_async_remote_copy(
                src_ref=mine.at[2 * n], dst_ref=red1.at[n, d - 1],
                send_sem=r1_snd.at[n], recv_sem=r1_rcv.at[n],
                device_id={"strip": wrap(strip + d, nz)}, device_id_type=MESH,
            ).start()
        if first_sent is not None:
            first_sent()
        wait_bytes(red1.at[n], r1_rcv.at[n])
        mine[2 * n + 1] = mine[2 * n] + jnp.sum(red1[n], axis=0)
        for d in range(ns - 1, 0, -1):
            pltpu.make_async_remote_copy(
                src_ref=mine.at[2 * n + 1], dst_ref=red2.at[n, d - 1],
                send_sem=r2_snd.at[n], recv_sem=r2_rcv.at[n],
                device_id={"sec": wrap(sec + d, ns)}, device_id_type=MESH,
            ).start()
        if second_sent is not None:
            second_sent()
        wait_bytes(red2.at[n], r2_rcv.at[n])
        whole = mine[2 * n + 1] + jnp.sum(red2[n], axis=0)
        wait_bytes(red1.at[n], r1_snd.at[n])
        wait_bytes(red2.at[n], r2_snd.at[n])
        power = jnp.sum(whole, axis=1, keepdims=True) * (1.0 / (STEP_SIZE * STEP_SIZE))
        spread = jnp.sqrt(power * (1.0 / entries) + EPSILON)
        scale = jnp.minimum(1.0, SPEED_CAP / spread)
        return jnp.broadcast_to(scale * DAMPING, (SUB, LANES))

    plain = DAMPING

    def wave(w, order, sweep, first_damping, own_rows, before=None, known=False):
        for k in range(SUBSTEPS):
            c = w - k
            last = k == SUBSTEPS - 1

            @pl.when(chunk_in(c))
            def _():
                if before is not None and k == 1:
                    before(c)
                if known and k == 0:
                    apply(c, order[0], pre, order[1], first_damping)
                else:
                    level(
                        k, c, order[k], order[k + 1], tgt[sweep],
                        first_damping if k == 0 else plain, own_rows and last, last,
                    )

    def boundary(sweep, c):
        for d in range(2):
            wait_bytes(rx.at[sweep, d, :, pl.ds(c * WIDE, WIDE), pl.ds(0, 2 * SUB)], e_rcv.at[d, c, 0])
        for p in range(2):
            make_target(sweep, c, *pieces[p])
        strip_start(t_halo(sweep, c))

    def interior(sweep, c):
        for d in range(2):
            wait_bytes(
                rx.at[sweep, d, :, pl.ds(c * WIDE, WIDE), pl.ds(SUB, rows - 2 * SUB)], e_rcv.at[d, c, 1]
            )
        make_target(sweep, c, *pieces[2])
        strip_wait_recv(t_halo(sweep, c))

    def sent(sweep):
        def before(c):
            for d in range(2):
                wait_bytes(rx.at[sweep, d, :, pl.ds(c * WIDE, WIDE)], e_snd.at[d, c])

        return before

    reset()
    strip_wait_send(u_halo)
    strip_wait_send(raw_halo)

    def round0(w, _):
        @pl.when(w < nc)
        def _():
            boundary(0, w)

        @pl.when(chunk_in(w - 1))
        def _():
            interior(0, w - 1)

        wave(w - 1, (sa, sb, sa, sb, sa), 0, None, False, before=sent(0))
        return 0

    lax.fori_loop(0, nc + SUBSTEPS, round0, 0)
    damping1 = spread_scale(0, lambda: forces(sa, 0))

    soon, ahead = min(3, nc), min(4, nc)

    def round1(w, _):
        wave(w, (sa, sb, sa, sb, sc), 0, damping1, True, known=True)
        c = w - (SUBSTEPS - 1)

        @pl.when(chunk_in(c))
        def _():
            make_down(1, c, sc)
            strip_start(s_halo(c))

        @pl.when(jnp.logical_and(c >= 0, c < soon))
        def _():
            e_send(1, c, sc)

        return 0

    lax.fori_loop(0, nc + SUBSTEPS - 1, round1, 0)

    def send_next():
        for c in range(soon, ahead):
            e_send(1, c, sc)

    def send_rest():
        def body(c, _):
            e_send(1, c, sc)
            return 0

        def early(c, _):
            boundary(1, c)
            return 0

        lax.fori_loop(ahead, nc, body, 0)
        lax.fori_loop(0, ahead, early, 0)

    damping2 = spread_scale(1, send_next, send_rest)

    reset()
    strip_wait_all(hears_from, sc.at[:, :, top_halo, :], h1_rcv)
    strip_wait_all(sends_to, sc.at[:, :, top_halo, :], h1_snd)

    def round2(w, _):
        @pl.when(jnp.logical_and(w >= ahead, w < nc))
        def _():
            boundary(1, w)

        @pl.when(chunk_in(w - 1))
        def _():
            interior(1, w - 1)

        wave(w - 1, (sc, sb, sc, sb, sc), 1, damping2, False, before=sent(1))
        return 0

    lax.fori_loop(0, nc + SUBSTEPS, round2, 0)
    damping_out[...] = spread_scale(2, lambda: forces(sc, 1))
    for sweep in range(2):
        strip_wait_all(sends_to, tgt[sweep].at[:, :, top_halo, :], th_snd.at[sweep])


def last_round(
    ns, rows, tiles_c,
    state, tgt, coef, pre, damping, out_u, out_v,
    sa, sb, stage, carry, out_sem,
):
    nc = tiles_c // WIDE
    level, apply = substeps(rows, tiles_c, coef, carry, None, pull_of(lax.axis_index("sec"), ns))
    clear_carry(carry, rows)
    first = damping[...]

    def wave(w, _):
        for k in range(SUBSTEPS):
            c = w - k

            @pl.when(jnp.logical_and(c >= 0, c < nc))
            def _():
                if k == 0:
                    apply(c, state, pre, sb, first)
                elif k == 1:
                    level(k, c, sb, sa, tgt, DAMPING, False)
                elif k == 2:
                    level(k, c, sa, sb, tgt, DAMPING, False)
                else:
                    level(k, c, sb, stage, tgt, DAMPING, True, mode="final")
                    for jj in range(WIDE):
                        j = c * WIDE + jj
                        cols = pl.ds(pl.multiple_of(j * LANES, LANES), LANES)
                        for n, out in enumerate((out_u, out_v)):
                            pltpu.make_async_copy(
                                stage.at[n, :, j], out.at[:, 0, :, cols], out_sem.at[0]
                            ).start()

        return 0

    lax.fori_loop(0, nc + SUBSTEPS - 1, wave, 0)
    pltpu.make_async_copy(stage, stage, out_sem.at[0]).wait()


def relax(mesh, start_offsets, section_flow, fixed_nodes, links_across, links_down):
    ns, nz = mesh.shape["sec"], mesh.shape["strip"]
    rows, columns = fixed_nodes.shape[1:]
    tiles_c = columns // LANES
    nc = tiles_c // WIDE
    padded = rows + 2 * HALO
    f32 = jnp.float32
    state = (4, tiles_c, padded + SUB, LANES)
    planes = lambda n: (n, tiles_c, padded, LANES)
    lines = pltpu.VMEM((SUBSTEPS, 2, padded, LANES), f32)
    dma = pltpu.SemaphoreType.DMA
    anywhere = pl.BlockSpec(memory_space=pltpu.HBM)
    near = pl.BlockSpec(memory_space=pltpu.VMEM)
    handed = (state, planes(2), planes(3), planes(2), (SUB, LANES))
    between = pl.pallas_call(
        functools.partial(kernel, ns, nz, rows, tiles_c),
        out_shape=tuple(pltpu.VMEM(shape, f32) for shape in handed),
        in_specs=[anywhere] * 5,
        out_specs=(near,) * len(handed),
        scratch_shapes=[
            pltpu.VMEM(state, f32),
            pltpu.VMEM(state, f32),
            pltpu.VMEM(planes(2), f32),
            pltpu.VMEM(planes(3), jnp.int32),
            pltpu.VMEM((2, tiles_c, rows, LANES), f32),
            pltpu.VMEM((2, 2, tiles_c, rows, LANES), f32),
            pltpu.VMEM((2, 2, 2, tiles_c, rows, LANES), f32),
            lines,
            pltpu.VMEM((SUB, LANES), f32),
            pltpu.VMEM((6, 1, LANES), f32),
            pltpu.VMEM((3, nz - 1, 1, LANES), f32),
            pltpu.VMEM((3, ns - 1, 1, LANES), f32),
            dma((nc,)), dma((1,)),
            dma((2, nc)), dma((2, nc, 2)),
            dma((2, 2)), dma((2, nc)),
            dma((2, 2)), dma((2, 2)),
            dma((2,)), dma((2,)),
            dma((3,)), dma((3,)), dma((3,)), dma((3,)),
        ],
        compiler_params=pltpu.CompilerParams(
            collective_id=0, has_side_effects=True, vmem_limit_bytes=107 * 512 * 1024
        ),
    )(start_offsets, section_flow, fixed_nodes, links_across, links_down)
    between = [pltpu.with_memory_space_constraint(x, pltpu.VMEM) for x in between]
    out = jax.ShapeDtypeStruct(start_offsets.shape, f32)
    return pl.pallas_call(
        functools.partial(last_round, ns, rows, tiles_c),
        out_shape=(out, out),
        in_specs=[near] * len(handed),
        out_specs=(anywhere, anywhere),
        scratch_shapes=[
            pltpu.VMEM(state, f32),
            pltpu.VMEM(state, f32),
            pltpu.VMEM((2, 2, tiles_c, rows, LANES), f32),
            lines,
            dma((1,)),
        ],
        compiler_params=pltpu.CompilerParams(
            vmem_limit_bytes=24 * 1024 * 1024
        ),
    )(*between)


def solution(mesh):
    whole = P(None, "sec", "strip", None)
    flags = P("sec", "strip", None)
    return jax.shard_map(
        functools.partial(relax, mesh),
        mesh=mesh,
        in_specs=(whole, whole, flags, flags, flags),
        out_specs=(whole, whole),
        check_vma=False,
    )
```
